128 devices in a mesh: row: 16 (over y, x), col: 8 (over z, core).
Axes of the slice: x: 4, y: 4, z: 4, core: 2. Of those that a mesh axis runs over, the one named last changes fastest.
Arguments:
- panel_cols: float32 [256, 16384], P('col', 'row'), as said below
- window_cols: float32 [16384, 16384], P('col', 'row'), may hold values from -6 to 6
Outputs:
- triangle: float32 [256, 256], replicated
- top_rows: float32 [16384, 256], P(('col', 'row'))
- residual: float32 [16384, 16384], P('col', 'row')
The draws below stay inside these ranges and needn't reach their ends.
Inputs may be any that keep to these rules, and one draw needn't show every extreme that they name: `panel_cols`: the 256 rows are linearly independent over the 1024 columns of every block of row.
All inputs are finite; a program needn't handle non-finite values.
Results may differ from the reference program's by a relative error of at most 0.000084.
Values sent between devices are 32-bit elements; how exact they have to be, the bound alone decides.
A program may use at most 64 MiB of HBM per device.

```python
import math
import jax
import jax.numpy as jnp
from jax import lax

PANEL = 256
WINDOW = 16384
ROWS = 16384


def draw_panel_cols(key, part):
    key_col = jax.random.fold_in(key, 11)
    key_row = jax.random.fold_in(key, 23)
    key_base = jax.random.fold_in(key, 37)
    column_scale = jnp.exp(jax.random.uniform(key_col, (PANEL, 1), jnp.float32) * math.log(10.0))
    row_scale = jnp.exp(jax.random.uniform(key_row, (1, ROWS), jnp.float32) * math.log(10.0))
    normal_part = jnp.clip(jax.random.normal(key_base, (PANEL, ROWS), jnp.float32), -6.0, 6.0)
    return (column_scale * row_scale * normal_part / math.sqrt(21.5 * ROWS)).astype(jnp.float32)


def raised(result, stream_key, source, target, shards_of, factor):
    owner, partner = [(jnp.arange(result.shape[dim]) // (result.shape[dim] // shards_of)).reshape([-1 if axis == dim else 1 for axis in range(result.ndim)]) for dim in (source, target)]
    chosen = jax.random.permutation(stream_key, shards_of)[partner]
    strong = (owner == chosen) | (owner == (partner + shards_of // 2) % shards_of)
    return jnp.where(strong, factor * result, result)


def shard_levels(stream_key, extent, pieces, smallest, largest):
    def one(axis_at, blocks):
        draws = jax.random.uniform(jax.random.fold_in(jax.random.fold_in(stream_key, 6), axis_at), (blocks,), jnp.float32, smallest / len(pieces), largest / len(pieces))
        return jnp.repeat(jnp.exp(draws), extent[axis_at] // blocks).reshape((-1,) + (1,) * (len(extent) - axis_at - 1))

    factor_of = one(*pieces[0])
    for cut in pieces[1:]:
        factor_of = factor_of * one(*cut)
    return factor_of


def noise_with(stream_key, dims, deviation, most, shards, heavy, kind=jnp.bfloat16):
    result = deviation * jax.random.normal(stream_key, dims, jnp.float32)
    if shards:
        result = result * shard_levels(stream_key, dims, shards, -0.22, 0.18)
    return jnp.clip(raised(result, jax.random.fold_in(stream_key, 3), *heavy), -most, most).astype(kind)


def setup_inputs(seed: int = 0) -> dict:
    streams_of = jax.random.split(jax.random.key(seed), 3)
    panel_cols = draw_panel_cols(jax.random.fold_in(streams_of[2], 71), 0)
    window_cols = noise_with(streams_of[1], (WINDOW, ROWS), 1.0, 6.0, ((0, 8), (1, 16)), (1, 0, 16, 2.0), jnp.float32)
    return dict(panel_cols=panel_cols, window_cols=window_cols)


def reference(panel_cols, window_cols):
    precise = lax.Precision.HIGHEST
    gram = jnp.dot(panel_cols.astype(jnp.float32), panel_cols.T.astype(jnp.float32), precision=precise, preferred_element_type=jnp.float32)
    lower_part = jnp.linalg.cholesky(gram)
    identity = jnp.eye(PANEL, dtype=jnp.float32)
    inverse = lax.linalg.triangular_solve(lower_part, identity, left_side=True, lower=True)
    cross = jnp.dot(window_cols.astype(jnp.float32), panel_cols.T.astype(jnp.float32), precision=precise, preferred_element_type=jnp.float32)
    top_rows = jnp.dot(cross.astype(jnp.float32), inverse.T.astype(jnp.float32), precision=precise, preferred_element_type=jnp.float32)
    combined = jnp.dot(top_rows.astype(jnp.float32), inverse.astype(jnp.float32), precision=precise, preferred_element_type=jnp.float32)
    residual = window_cols - jnp.dot(combined.astype(jnp.float32), panel_cols.astype(jnp.float32), precision=precise, preferred_element_type=jnp.float32)
    return (lower_part.T, top_rows, residual)
```

```python
import jax
import jax.numpy as jnp
from jax import lax
from jax.experimental import pallas as pl
from jax.experimental.pallas import tpu as pltpu
from jax.sharding import PartitionSpec as P

MESH = pl.DeviceIdType.MESH
HIGHEST = lax.Precision.HIGHEST
F32 = jnp.float32
BF16 = jnp.bfloat16

N = 256
SLAB = 2048
DEPTH = 1024
PIECE = 32
CHUNKS = 2
S1 = 256 // CHUNKS
S2 = S1 // 4
BLOCK = 32


def dot_nt(a, b, precision=None):
    return lax.dot_general(a, b, (((1,), (1,)), ((), ())), precision=precision, preferred_element_type=F32)


def dot_nn(a, b, precision=None):
    return lax.dot_general(a, b, (((1,), (0,)), ((), ())), precision=precision, preferred_element_type=F32)


def dot_tn(a, b, precision=None):
    return lax.dot_general(a, b, (((0,), (0,)), ((), ())), precision=precision, preferred_element_type=F32)


def split(v):
    high = v.astype(BF16)
    return high, (v - high.astype(F32)).astype(BF16)


N_PANEL = 13
N_GRAM = 13
N_CROSS = 2 * CHUNKS * 24


def body(
    panel_ref, w_hbm,
    u_out, top_out, ch_out, cl_out, bh_out, bl_out,
    w_ref, wh_ref, wl_ref, a_ref, ah_ref, al_ref, gx_ref, gy_ref, gz_ref, t_ref,
    c_ref, f_ref, r1_ref, r2_ref, w_sem, send_sem, recv_sem,
):
    row = lax.axis_index("row")
    col = lax.axis_index("col")
    y, x = lax.div(row, 4), lax.rem(row, 4)
    z, k = lax.div(col, 2), lax.rem(col, 2)

    def step(v, d):
        return lax.rem(v + d, 4)

    def at_x(d):
        return (y * 4 + step(x, d), col)

    def at_y(d):
        return (step(y, d) * 4 + x, col)

    def piece(d, core):
        return step(z, d) * 2 + core

    partner = (row, z * 2 + 1 - k)
    up, down = (row, piece(1, k)), (row, piece(3, k))

    for b in range(8):
        pltpu.make_async_copy(w_hbm.at[pl.ds(b * 256, 256), :], w_ref.at[pl.ds(b * 256, 256), :], w_sem.at[b]).start()

    barrier = pltpu.get_barrier_semaphore()
    others = [at_x(d) for d in (1, 2, 3)] + [at_y(d) for d in (1, 2, 3)]
    others += [(row, lax.rem(col + d, 8)) for d in range(1, 8)]
    for dev in others:
        pl.semaphore_signal(barrier, inc=1, device_id=dev, device_id_type=MESH)
    pl.semaphore_wait(barrier, len(others))

    sent = []

    def send(index, src, dst, dev):
        copy = pltpu.make_async_remote_copy(
            src_ref=src, dst_ref=dst, send_sem=send_sem.at[index], recv_sem=recv_sem.at[index],
            device_id=dev, device_id_type=MESH,
        )
        copy.start()
        sent.append(copy)
        return copy

    half = (pl.ds(0, 16), pl.ds(16, 16))
    own = {}
    own["up0"] = send(0, panel_ref.at[half[0]], a_ref.at[col, half[0]], up)
    own["down1"] = send(1, panel_ref.at[half[1]], a_ref.at[col, half[1]], down)
    own["up1"] = send(2, panel_ref.at[half[1]], a_ref.at[col, half[1]], up)
    own["down0"] = send(3, panel_ref.at[half[0]], a_ref.at[col, half[0]], down)
    own["partner"] = send(4, panel_ref, a_ref.at[col], partner)
    a_ref[col] = panel_ref[...]

    for b in range(8):
        rows = pl.ds(b * 256, 256)
        pltpu.make_async_copy(w_hbm.at[rows, :], w_ref.at[rows, :], w_sem.at[b]).wait()
        high, low = split(w_ref[rows, :])
        wh_ref[rows, :] = high
        wl_ref[rows, :] = low

    below, above, far = piece(3, k), piece(1, k), piece(2, k)

    def pass_on(index, who, h, dev):
        return send(index, a_ref.at[who, half[h]], a_ref.at[who, half[h]], dev)

    own["up0"].wait_recv()
    relay0 = pass_on(5, below, 0, up)
    own["down1"].wait_recv()
    relay1 = pass_on(6, above, 1, down)
    forwards = [pass_on(7, below, 0, partner), pass_on(8, above, 1, partner)]
    own["up1"].wait_recv()
    forwards.append(pass_on(9, below, 1, partner))
    own["down0"].wait_recv()
    forwards.append(pass_on(10, above, 0, partner))
    relay0.wait_recv()
    forwards.append(pass_on(11, far, 0, partner))
    relay1.wait_recv()
    forwards.append(pass_on(12, far, 1, partner))
    own["partner"].wait_recv()
    for copy in forwards:
        copy.wait_recv()

    panel = a_ref[...].reshape(N, DEPTH)
    high, low = split(panel)
    ah_ref[...] = high
    al_ref[...] = low

    base = N_PANEL
    gx_ref[x] = dot_nt(panel_ref[...], panel, HIGHEST)
    gram_x = [send(base + d - 1, gx_ref.at[x], gx_ref.at[x], at_x(d)) for d in (1, 2, 3)]

    def gram_to_y():
        for copy in gram_x:
            copy.wait_recv()
        gy_ref[y] = (gx_ref[0] + gx_ref[1]) + (gx_ref[2] + gx_ref[3])
        return [send(base + 3 + d - 1, gy_ref.at[y], gy_ref.at[y], at_y(d)) for d in (1, 2, 3)]

    def gram_to_col(gram_y):
        for copy in gram_y:
            copy.wait_recv()
        gz_ref[col] = (gy_ref[0] + gy_ref[1]) + (gy_ref[2] + gy_ref[3])
        return [send(base + 6 + d - 1, gz_ref.at[col], gz_ref.at[col], (row, lax.rem(col + d, 8))) for d in range(1, 8)]

    def gram_done(gram_z):
        for copy in gram_z:
            copy.wait_recv()
        t_ref[:, :N] = gz_ref[...].reshape(N, N)
        rows_at = lax.broadcasted_iota(jnp.int32, (N, N), 0)
        cols_at = lax.broadcasted_iota(jnp.int32, (N, N), 1)
        t_ref[:, N:] = jnp.where(rows_at == cols_at, 1.0, 0.0).astype(F32)

    def factor(b):
        lo = b * BLOCK
        tile, shift = lo // 128 * 128, lo % 128
        e = t_ref[lo:lo + BLOCK, tile:tile + 128]
        if shift:
            e = pltpu.roll(e, 128 - shift, 1)
        sub = lax.broadcasted_iota(jnp.int32, (BLOCK, 128), 0)
        lane = lax.broadcasted_iota(jnp.int32, (BLOCK, 128), 1)
        e = jnp.where(lane < BLOCK, e, jnp.where(lane == sub + BLOCK, 1.0, 0.0).astype(F32))
        for j in range(BLOCK - 1):
            pivot_row = e[j:j + 1, :]
            pivot = jnp.broadcast_to(pivot_row[:, j:j + 1], (1, 128))
            column = jnp.broadcast_to(e[:, j:j + 1], (BLOCK, 128))
            e = e - jnp.where(sub > j, column, 0.0) * (pivot_row / pivot)
        diagonal = jnp.sum(jnp.where(lane == sub, e, 0.0), axis=1, keepdims=True)
        root = lax.rsqrt(diagonal)
        root = root * (1.5 - 0.5 * diagonal * root * root)
        e = e * root
        inverse = e[:, BLOCK:2 * BLOCK]
        done = dot_nn(inverse, t_ref[lo:lo + BLOCK, :], HIGHEST)
        t_ref[lo:lo + BLOCK, :] = done
        if lo + BLOCK < N:
            update = dot_tn(done[:, :N], done, HIGHEST)
            t_ref[lo + BLOCK:, :] -= update[lo + BLOCK:, :]

    def finish():
        rows_at = lax.broadcasted_iota(jnp.int32, (N, N), 0)
        cols_at = lax.broadcasted_iota(jnp.int32, (N, N), 1)
        u_out[...] = jnp.where(cols_at >= rows_at, t_ref[:, :N], 0.0)
        inverse = jnp.where(cols_at <= rows_at, t_ref[:, N:], 0.0)
        t_ref[:, N:] = inverse
        q = dot_nn(inverse, a_ref[...].reshape(N, DEPTH), HIGHEST)
        high, low = split(dot_tn(inverse, q, HIGHEST))
        bh_ref, bl_ref = bh_out, bl_out
        bh_ref[...] = high
        bl_ref[...] = low

    def rows_of(start, size, align):
        return pl.ds(pl.multiple_of(start, align), size)

    def product(part, d):
        where = rows_of(part * 1024 + step(y if part else x, d) * 256, 256, 256)
        wh, wl = wh_ref[where, :], wl_ref[where, :]
        ah, al = ah_ref[...], al_ref[...]
        c_ref[where, :] = (dot_nt(wh, al) + dot_nt(wl, ah)) + dot_nt(wh, ah)

    class Stream:
        def __init__(self, part, chunk):
            self.at = (at_y, at_x) if part else (at_x, at_y)
            self.me = (y, x) if part else (x, y)
            self.start = part * 1024 + chunk * S1
            self.index = N_PANEL + N_GRAM + (part * CHUNKS + chunk) * 24
            self.buf = (r1_ref.at[part, chunk], r2_ref.at[part, chunk])

        def place(self, axis, d, h, buf_rows=None):
            size = S2 if axis else S1
            start = self.start + self.me[0] * 256
            if axis:
                start = start + step(self.me[1], d) * S2
            else:
                start = self.start + step(self.me[0], d) * 256
            if h is None:
                return rows_of(start, size, size)
            return rows_of(start + h * (size // 2), size // 2, size // 2)

        def rs_send(self, axis, slot, src, d):
            return send(self.index + axis * 6 + slot, c_ref.at[src, :], self.buf[axis].at[slot], self.at[axis](d))

        def far_out(self, axis):
            self.rs = [None] * 6
            self.rs[0] = self.rs_send(axis, 0, self.place(axis, 2, 0), 1)
            self.rs[1] = self.rs_send(axis, 1, self.place(axis, 2, 1), 3)

        def near_out(self, axis):
            self.rs[2] = self.rs_send(axis, 2, self.place(axis, 1, 1), 1)
            self.rs[3] = self.rs_send(axis, 3, self.place(axis, 3, 0), 3)

        def relay(self, axis):
            for slot, (d, h) in enumerate(((1, 0), (3, 1))):
                self.rs[slot].wait_recv()
                where = self.place(axis, d, h)
                c_ref[where, :] += self.buf[axis][slot]
                self.rs[4 + slot] = self.rs_send(axis, 4 + slot, where, d)

        def gathered(self, axis, into):
            for slot in (2, 3, 4, 5):
                self.rs[slot].wait_recv()
            for h, (a, b) in enumerate(((3, 4), (2, 5))):
                where = self.place(axis, 0, h)
                into[where, :] = c_ref[where, :] + (self.buf[axis][a] + self.buf[axis][b])

        def ag_send(self, axis, slot, where, d):
            return send(self.index + 12 + axis * 6 + slot, f_ref.at[where, :], f_ref.at[where, :], self.at[axis](d))

        def spread(self, axis):
            self.ag = [
                self.ag_send(axis, 0, self.place(axis, 0, 0), 1),
                self.ag_send(axis, 1, self.place(axis, 0, 1), 3),
                self.ag_send(axis, 2, self.place(axis, 0, 1), 1),
                self.ag_send(axis, 3, self.place(axis, 0, 0), 3),
            ]

        def hand_on(self, axis):
            self.ag[0].wait_recv()
            self.ag.append(self.ag_send(axis, 4, self.place(axis, 3, 0), 1))
            self.ag[1].wait_recv()
            self.ag.append(self.ag_send(axis, 5, self.place(axis, 1, 1), 3))

        def spread_done(self, axis):
            for slot in (2, 3, 4, 5):
                self.ag[slot].wait_recv()

    streams = [[Stream(part, chunk) for part in range(2)] for chunk in range(CHUNKS)]

    def run(chunk, number):
        for s in streams[chunk]:
            if number == 0:
                s.far_out(0)
            elif number == 1:
                s.near_out(0)
            elif number == 2:
                s.relay(0)
            elif number == 3:
                s.gathered(0, c_ref)
                s.far_out(1)
                s.near_out(1)
            elif number == 4:
                s.relay(1)
            elif number == 5:
                s.gathered(1, f_ref)
                s.spread(1)
            elif number == 6:
                s.hand_on(1)
            elif number == 7:
                s.spread_done(1)
                s.spread(0)
            elif number == 8:
                s.hand_on(0)
            elif number == 9:
                s.spread_done(0)

    product(0, 2)
    product(1, 2)
    run(0, 0)
    gram_y = gram_to_y()
    run(1, 0)
    for d in (1, 3):
        product(0, d)
        product(1, d)
    run(0, 1)
    gram_z = gram_to_col(gram_y)
    run(1, 1)
    product(0, 0)
    product(1, 0)
    run(0, 2)
    gram_done(gram_z)
    factor(0)
    run(1, 2)
    for number in range(3, 9):
        run(0, number)
        factor(number - 2)
        run(1, number)
    factor(7)
    run(0, 9)
    finish()
    run(1, 9)

    for b in range(8):
        rows = pl.ds(b * 256, 256)
        high, low = split(f_ref[rows, :])
        ch_out[rows, :] = high
        cl_out[rows, :] = low
    top_out[...] = dot_nt(f_ref[rows_of(row * 128, 128, 128), :], t_ref[:, N:], HIGHEST)

    for copy in sent:
        copy.wait_send()


def gather_and_factor(panel_cols, window_cols):
    vmem = pl.BlockSpec(memory_space=pltpu.VMEM)
    count = N_PANEL + N_GRAM + N_CROSS
    return pl.pallas_call(
        body,
        out_shape=(
            jax.ShapeDtypeStruct((N, N), F32),
            jax.ShapeDtypeStruct((128, N), F32),
            jax.ShapeDtypeStruct((SLAB, N), BF16),
            jax.ShapeDtypeStruct((SLAB, N), BF16),
            jax.ShapeDtypeStruct((N, DEPTH), BF16),
            jax.ShapeDtypeStruct((N, DEPTH), BF16),
        ),
        in_specs=[vmem, pl.BlockSpec(memory_space=pl.ANY)],
        out_specs=(vmem,) * 6,
        scratch_shapes=[
            pltpu.VMEM((SLAB, DEPTH), F32),
            pltpu.VMEM((SLAB, DEPTH), BF16),
            pltpu.VMEM((SLAB, DEPTH), BF16),
            pltpu.VMEM((8, PIECE, DEPTH), F32),
            pltpu.VMEM((N, DEPTH), BF16),
            pltpu.VMEM((N, DEPTH), BF16),
            pltpu.VMEM((4, PIECE, N), F32),
            pltpu.VMEM((4, PIECE, N), F32),
            pltpu.VMEM((8, PIECE, N), F32),
            pltpu.VMEM((N, 2 * N), F32),
            pltpu.VMEM((SLAB, N), F32),
            pltpu.VMEM((SLAB, N), F32),
            pltpu.VMEM((2, CHUNKS, 6, S1 // 2, N), F32),
            pltpu.VMEM((2, CHUNKS, 6, S2 // 2, N), F32),
            pltpu.SemaphoreType.DMA((8,)),
            pltpu.SemaphoreType.DMA((count,)),
            pltpu.SemaphoreType.DMA((count,)),
        ],
        compiler_params=pltpu.CompilerParams(
            collective_id=0, has_side_effects=True, vmem_limit_bytes=56 * 2**20
        ),
        name="gather_and_factor",
    )(panel_cols, window_cols)


def residual_body(w_ref, ch_ref, cl_ref, bh_ref, bl_ref, out_ref):
    ch, cl, bh, bl = ch_ref[...], cl_ref[...], bh_ref[...], bl_ref[...]
    out_ref[...] = w_ref[...] - ((dot_nn(ch, bl) + dot_nn(cl, bh)) + dot_nn(ch, bh))


def subtract(window_cols, ch, cl, bh, bl):
    rows = 256
    return pl.pallas_call(
        residual_body,
        out_shape=jax.ShapeDtypeStruct((SLAB, DEPTH), F32),
        grid=(SLAB // rows,),
        in_specs=[
            pl.BlockSpec((rows, DEPTH), lambda i: (i, 0)),
            pl.BlockSpec((rows, N), lambda i: (i, 0)),
            pl.BlockSpec((rows, N), lambda i: (i, 0)),
            pl.BlockSpec((N, DEPTH), lambda i: (0, 0)),
            pl.BlockSpec((N, DEPTH), lambda i: (0, 0)),
        ],
        out_specs=pl.BlockSpec((rows, DEPTH), lambda i: (i, 0)),
        name="subtract",
    )(window_cols, ch, cl, bh, bl)


def local(panel_cols, window_cols):
    triangle, top_rows, ch, cl, bh, bl = gather_and_factor(panel_cols, window_cols)
    residual = subtract(window_cols, ch, cl, bh, bl)
    return triangle, top_rows, residual


def solution(mesh):
    return jax.shard_map(
        local,
        mesh=mesh,
        in_specs=(P("col", "row"), P("col", "row")),
        out_specs=(P(), P(("col", "row"), None), P("col", "row")),
        check_vma=False,
    )
```

```python
import jax
import jax.numpy as jnp
from jax import lax
from jax.experimental import pallas as pl
from jax.experimental.pallas import tpu as pltpu
from jax.sharding import PartitionSpec as P

MESH = pl.DeviceIdType.MESH
HIGHEST = lax.Precision.HIGHEST
F32 = jnp.float32
BF16 = jnp.bfloat16

N = 256
SLAB = 2048
DEPTH = 1024
PIECE = 32
CHUNKS = 2
S1 = 256 // CHUNKS
S2 = S1 // 4
BLOCK = 64
TILES = 8


def dot_nt(a, b, precision=None):
    return lax.dot_general(a, b, (((1,), (1,)), ((), ())), precision=precision, preferred_element_type=F32)


def dot_nn(a, b, precision=None):
    return lax.dot_general(a, b, (((1,), (0,)), ((), ())), precision=precision, preferred_element_type=F32)


def dot_tn(a, b, precision=None):
    return lax.dot_general(a, b, (((0,), (0,)), ((), ())), precision=precision, preferred_element_type=F32)


def split(v):
    high = v.astype(BF16)
    return high, (v - high.astype(F32)).astype(BF16)


N_PANEL = 13
N_GRAM = 13
N_CROSS = 2 * CHUNKS * 24


def body(
    panel_ref, w_hbm,
    u_out, top_out, w_ref, f_ref, bh_out, bl_out,
    wh_ref, wl_ref, a_ref, ah_ref, al_ref, gx_ref, gy_ref, gz_ref, t_ref,
    c_ref, r1_ref, r2_ref, w_sem, send_sem, recv_sem,
):
    row = lax.axis_index("row")
    col = lax.axis_index("col")
    y, x = lax.div(row, 4), lax.rem(row, 4)
    z, k = lax.div(col, 2), lax.rem(col, 2)

    def step(v, d):
        return lax.rem(v + d, 4)

    def at_x(d):
        return (y * 4 + step(x, d), col)

    def at_y(d):
        return (step(y, d) * 4 + x, col)

    def piece(d, core):
        return step(z, d) * 2 + core

    partner = (row, z * 2 + 1 - k)
    up, down = (row, piece(1, k)), (row, piece(3, k))

    for b in range(8):
        pltpu.make_async_copy(w_hbm.at[pl.ds(b * 256, 256), :], w_ref.at[pl.ds(b * 256, 256), :], w_sem.at[b]).start()

    barrier = pltpu.get_barrier_semaphore()
    others = [at_x(d) for d in (1, 2, 3)] + [at_y(d) for d in (1, 2, 3)]
    others += [(row, lax.rem(col + d, 8)) for d in range(1, 8)]
    for dev in others:
        pl.semaphore_signal(barrier, inc=1, device_id=dev, device_id_type=MESH)
    pl.semaphore_wait(barrier, len(others))

    sent = []

    def send(index, src, dst, dev):
        copy = pltpu.make_async_remote_copy(
            src_ref=src, dst_ref=dst, send_sem=send_sem.at[index], recv_sem=recv_sem.at[index],
            device_id=dev, device_id_type=MESH,
        )
        copy.start()
        sent.append(copy)
        return copy

    half = (pl.ds(0, 16), pl.ds(16, 16))
    own = {}
    own["up0"] = send(0, panel_ref.at[half[0]], a_ref.at[col, half[0]], up)
    own["down1"] = send(1, panel_ref.at[half[1]], a_ref.at[col, half[1]], down)
    own["up1"] = send(2, panel_ref.at[half[1]], a_ref.at[col, half[1]], up)
    own["down0"] = send(3, panel_ref.at[half[0]], a_ref.at[col, half[0]], down)
    own["partner"] = send(4, panel_ref, a_ref.at[col], partner)
    a_ref[col] = panel_ref[...]

    for b in range(8):
        rows = pl.ds(b * 256, 256)
        pltpu.make_async_copy(w_hbm.at[rows, :], w_ref.at[rows, :], w_sem.at[b]).wait()
        high, low = split(w_ref[rows, :])
        wh_ref[rows, :] = high
        wl_ref[rows, :] = low

    below, above, far = piece(3, k), piece(1, k), piece(2, k)

    def pass_on(index, who, h, dev):
        return send(index, a_ref.at[who, half[h]], a_ref.at[who, half[h]], dev)

    gram_blocks = [None] * 4

    def pair_here(d):
        first = step(z, d) * 2
        pair = a_ref[pl.ds(first, 2)].reshape(2 * PIECE, DEPTH)
        where = pl.ds(pl.multiple_of(first * PIECE, 2 * PIECE), 2 * PIECE)
        high, low = split(pair)
        ah_ref[where, :] = high
        al_ref[where, :] = low
        gram_blocks[d] = dot_nt(panel_ref[...], pair, HIGHEST)

    own["up0"].wait_recv()
    relay0 = pass_on(5, below, 0, up)
    own["down1"].wait_recv()
    relay1 = pass_on(6, above, 1, down)
    forwards = [pass_on(7, below, 0, partner), pass_on(8, above, 1, partner)]
    own["partner"].wait_recv()
    pair_here(0)
    own["up1"].wait_recv()
    forwards.append(pass_on(9, below, 1, partner))
    own["down0"].wait_recv()
    forwards.append(pass_on(10, above, 0, partner))
    for copy in forwards:
        copy.wait_recv()
    pair_here(1)
    pair_here(3)
    relay0.wait_recv()
    forwards.append(pass_on(11, far, 0, partner))
    relay1.wait_recv()
    forwards.append(pass_on(12, far, 1, partner))
    for copy in forwards[4:]:
        copy.wait_recv()
    pair_here(2)

    base = N_PANEL
    gx_ref[x] = pltpu.roll(jnp.concatenate(gram_blocks, axis=1), z * 2 * PIECE, 1)
    gram_x = [send(base + d - 1, gx_ref.at[x], gx_ref.at[x], at_x(d)) for d in (1, 2, 3)]

    def gram_to_y():
        for copy in gram_x:
            copy.wait_recv()
        gy_ref[y] = (gx_ref[0] + gx_ref[1]) + (gx_ref[2] + gx_ref[3])
        return [send(base + 3 + d - 1, gy_ref.at[y], gy_ref.at[y], at_y(d)) for d in (1, 2, 3)]

    def gram_to_col(gram_y):
        for copy in gram_y:
            copy.wait_recv()
        gz_ref[col] = (gy_ref[0] + gy_ref[1]) + (gy_ref[2] + gy_ref[3])
        return [send(base + 6 + d - 1, gz_ref.at[col], gz_ref.at[col], (row, lax.rem(col + d, 8))) for d in range(1, 8)]

    def gram_done(gram_z):
        for copy in gram_z:
            copy.wait_recv()
        t_ref[:, :N] = gz_ref[...].reshape(N, N)
        rows_at = lax.broadcasted_iota(jnp.int32, (N, N), 0)
        cols_at = lax.broadcasted_iota(jnp.int32, (N, N), 1)
        t_ref[:, N:] = jnp.where(rows_at == cols_at, 1.0, 0.0).astype(F32)

    sub = lax.broadcasted_iota(jnp.int32, (BLOCK, 128), 0)
    lane = lax.broadcasted_iota(jnp.int32, (BLOCK, 128), 1)
    state = [None]

    def pivots(b, first, last):
        lo = b * BLOCK
        if first == 0:
            tile, shift = lo // 128 * 128, lo % 128
            e = t_ref[lo:lo + BLOCK, tile:tile + 128]
            if shift:
                e = pltpu.roll(e, 128 - shift, 1)
            e = jnp.where(lane < BLOCK, e, jnp.where(lane == sub + BLOCK, 1.0, 0.0).astype(F32))
        else:
            e = state[0]
        for j in range(first, last, 2):
            r0, r1 = e[j:j + 1, :], e[j + 1:j + 2, :]
            c0 = jnp.broadcast_to(e[:, j:j + 1], (BLOCK, 128))
            c1 = jnp.broadcast_to(e[:, j + 1:j + 2], (BLOCK, 128))
            p, q, r = c0[j:j + 1, :], c1[j:j + 1, :], c1[j + 1:j + 2, :]
            over = 1.0 / (p * r - q * q)
            w0, w1 = (r * r0 - q * r1) * over, (p * r1 - q * r0) * over
            change = jnp.where(sub > j + 1, c0 * w0 + c1 * w1, 0.0)
            change = jnp.where(sub == j + 1, q * (r0 / p), change)
            e = e - change
        state[0] = e

    def apply(b):
        lo = b * BLOCK
        e = state[0]
        diagonal = jnp.sum(jnp.where(lane == sub, e, 0.0), axis=1, keepdims=True)
        root = lax.rsqrt(diagonal)
        root = root * (1.5 - 0.5 * diagonal * root * root)
        inverse = (e * root)[:, BLOCK:2 * BLOCK]
        done = dot_nn(inverse, t_ref[lo:lo + BLOCK, :], HIGHEST)
        t_ref[lo:lo + BLOCK, :] = done
        if lo + BLOCK < N:
            update = dot_tn(done[:, :N], done, HIGHEST)
            t_ref[lo + BLOCK:, :] -= update[lo + BLOCK:, :]

    def finish():
        rows_at = lax.broadcasted_iota(jnp.int32, (N, N), 0)
        cols_at = lax.broadcasted_iota(jnp.int32, (N, N), 1)
        u_out[...] = jnp.where(cols_at >= rows_at, t_ref[:, :N], 0.0)
        inverse = jnp.where(cols_at <= rows_at, t_ref[:, N:], 0.0)
        t_ref[:, N:] = inverse
        q = dot_nn(inverse, a_ref[...].reshape(N, DEPTH), HIGHEST)
        high, low = split(dot_tn(inverse, q, HIGHEST))
        bh_out[...] = high
        bl_out[...] = low

    pieces = []
    for b in range(N // BLOCK):
        pieces.append(lambda b=b: pivots(b, 0, BLOCK // 2))
        pieces.append(lambda b=b: (pivots(b, BLOCK // 2, BLOCK), apply(b)))

    def rows_of(start, size, align):
        return pl.ds(pl.multiple_of(start, align), size)

    def product(part, d):
        where = rows_of(part * 1024 + step(y if part else x, d) * 256, 256, 256)
        wh, wl = wh_ref[where, :], wl_ref[where, :]
        ah, al = ah_ref[...], al_ref[...]
        c_ref[where, :] = (dot_nt(wh, al) + dot_nt(wl, ah)) + dot_nt(wh, ah)

    class Stream:
        def __init__(self, part, chunk):
            self.at = (at_y, at_x) if part else (at_x, at_y)
            self.me = (y, x) if part else (x, y)
            self.start = part * 1024 + chunk * S1
            self.index = N_PANEL + N_GRAM + (part * CHUNKS + chunk) * 24
            self.buf = (r1_ref.at[part, chunk], r2_ref.at[part, chunk])

        def place(self, axis, d, h, buf_rows=None):
            size = S2 if axis else S1
            start = self.start + self.me[0] * 256
            if axis:
                start = start + step(self.me[1], d) * S2
            else:
                start = self.start + step(self.me[0], d) * 256
            if h is None:
                return rows_of(start, size, size)
            return rows_of(start + h * (size // 2), size // 2, size // 2)

        def rs_send(self, axis, slot, src, d):
            return send(self.index + axis * 6 + slot, c_ref.at[src, :], self.buf[axis].at[slot], self.at[axis](d))

        def far_out(self, axis):
            self.rs = [None] * 6
            self.rs[0] = self.rs_send(axis, 0, self.place(axis, 2, 0), 1)
            self.rs[1] = self.rs_send(axis, 1, self.place(axis, 2, 1), 3)

        def near_out(self, axis):
            self.rs[2] = self.rs_send(axis, 2, self.place(axis, 1, 1), 1)
            self.rs[3] = self.rs_send(axis, 3, self.place(axis, 3, 0), 3)

        def relay(self, axis):
            for slot, (d, h) in enumerate(((1, 0), (3, 1))):
                self.rs[slot].wait_recv()
                where = self.place(axis, d, h)
                c_ref[where, :] += self.buf[axis][slot]
                self.rs[4 + slot] = self.rs_send(axis, 4 + slot, where, d)

        def gathered(self, axis, into):
            for slot in (2, 3, 4, 5):
                self.rs[slot].wait_recv()
            for h, (a, b) in enumerate(((3, 4), (2, 5))):
                where = self.place(axis, 0, h)
                into[where, :] = c_ref[where, :] + (self.buf[axis][a] + self.buf[axis][b])

        def ag_send(self, axis, slot, where, d):
            return send(self.index + 12 + axis * 6 + slot, f_ref.at[where, :], f_ref.at[where, :], self.at[axis](d))

        def spread(self, axis):
            self.ag = [
                self.ag_send(axis, 0, self.place(axis, 0, 0), 1),
                self.ag_send(axis, 1, self.place(axis, 0, 1), 3),
                self.ag_send(axis, 2, self.place(axis, 0, 1), 1),
                self.ag_send(axis, 3, self.place(axis, 0, 0), 3),
            ]

        def hand_on(self, axis):
            self.ag[0].wait_recv()
            self.ag.append(self.ag_send(axis, 4, self.place(axis, 3, 0), 1))
            self.ag[1].wait_recv()
            self.ag.append(self.ag_send(axis, 5, self.place(axis, 1, 1), 3))

        def spread_done(self, axis):
            for slot in (2, 3, 4, 5):
                self.ag[slot].wait_recv()

    streams = [[Stream(part, chunk) for part in range(2)] for chunk in range(CHUNKS)]

    def run(chunk, number):
        for s in streams[chunk]:
            if number == 0:
                s.far_out(0)
            elif number == 1:
                s.near_out(0)
            elif number == 2:
                s.relay(0)
            elif number == 3:
                s.gathered(0, c_ref)
                s.far_out(1)
                s.near_out(1)
            elif number == 4:
                s.relay(1)
            elif number == 5:
                s.gathered(1, f_ref)
                s.spread(1)
            elif number == 6:
                s.hand_on(1)
            elif number == 7:
                s.spread_done(1)
                s.spread(0)
            elif number == 8:
                s.hand_on(0)
            elif number == 9:
                s.spread_done(0)

    product(0, 2)
    product(1, 2)
    run(0, 0)
    gram_y = gram_to_y()
    run(1, 0)
    for d in (1, 3):
        product(0, d)
        product(1, d)
    run(0, 1)
    gram_z = gram_to_col(gram_y)
    run(1, 1)
    product(0, 0)
    product(1, 0)
    run(0, 2)
    gram_done(gram_z)
    pieces[0]()
    run(1, 2)
    for number in range(3, 9):
        run(0, number)
        pieces[number - 2]()
        run(1, number)
    pieces[7]()
    run(0, 9)
    finish()
    run(1, 9)
    top_out[...] = dot_nt(f_ref[rows_of(row * 128, 128, 128), :], t_ref[:, N:], HIGHEST)

    for copy in sent:
        copy.wait_send()


def gather_and_factor(panel_cols, window_cols):
    vmem = pl.BlockSpec(memory_space=pltpu.VMEM)
    count = N_PANEL + N_GRAM + N_CROSS
    return pl.pallas_call(
        body,
        out_shape=(
            pltpu.VMEM((N, N), F32),
            pltpu.VMEM((128, N), F32),
            pltpu.VMEM((SLAB, DEPTH), F32),
            pltpu.VMEM((SLAB, N), F32),
            pltpu.VMEM((N, DEPTH), BF16),
            pltpu.VMEM((N, DEPTH), BF16),
        ),
        in_specs=[vmem, pl.BlockSpec(memory_space=pl.ANY)],
        out_specs=(vmem,) * 6,
        scratch_shapes=[
            pltpu.VMEM((SLAB, DEPTH), BF16),
            pltpu.VMEM((SLAB, DEPTH), BF16),
            pltpu.VMEM((8, PIECE, DEPTH), F32),
            pltpu.VMEM((N, DEPTH), BF16),
            pltpu.VMEM((N, DEPTH), BF16),
            pltpu.VMEM((4, PIECE, N), F32),
            pltpu.VMEM((4, PIECE, N), F32),
            pltpu.VMEM((8, PIECE, N), F32),
            pltpu.VMEM((N, 2 * N), F32),
            pltpu.VMEM((SLAB, N), F32),
            pltpu.VMEM((2, CHUNKS, 6, S1 // 2, N), F32),
            pltpu.VMEM((2, CHUNKS, 6, S2 // 2, N), F32),
            pltpu.SemaphoreType.DMA((8,)),
            pltpu.SemaphoreType.DMA((count,)),
            pltpu.SemaphoreType.DMA((count,)),
        ],
        compiler_params=pltpu.CompilerParams(
            collective_id=0, has_side_effects=True, vmem_limit_bytes=36 * 2**20
        ),
        name="gather_and_factor",
    )(panel_cols, window_cols)


def subtract_body(u_ref, top_ref, w_ref, f_ref, bh_ref, bl_ref, u_out, top_out, out, r_ref, sem, side_sem):
    sides = [
        pltpu.make_async_copy(u_ref, u_out, side_sem.at[0]),
        pltpu.make_async_copy(top_ref, top_out, side_sem.at[1]),
    ]
    for copy in sides:
        copy.start()
    rows = SLAB // TILES
    copies = []
    for b in range(TILES):
        where = pl.ds(b * rows, rows)
        fh, fl = split(f_ref[where, :])
        bh = bh_ref[...]
        r_ref[where, :] = w_ref[where, :] - ((dot_nn(fh, bl_ref[...]) + dot_nn(fl, bh)) + dot_nn(fh, bh))
        copies.append(pltpu.make_async_copy(r_ref.at[where, :], out.at[where, :], sem.at[b]))
        copies[-1].start()
    for copy in sides + copies:
        copy.wait()


def subtract(*given):
    vmem = pl.BlockSpec(memory_space=pltpu.VMEM)
    anywhere = pl.BlockSpec(memory_space=pl.ANY)
    return pl.pallas_call(
        subtract_body,
        out_shape=(
            jax.ShapeDtypeStruct((N, N), F32),
            jax.ShapeDtypeStruct((128, N), F32),
            jax.ShapeDtypeStruct((SLAB, DEPTH), F32),
        ),
        in_specs=[vmem] * 6,
        out_specs=(anywhere,) * 3,
        scratch_shapes=[
            pltpu.VMEM((SLAB, DEPTH), F32),
            pltpu.SemaphoreType.DMA((TILES,)),
            pltpu.SemaphoreType.DMA((2,)),
        ],
        compiler_params=pltpu.CompilerParams(vmem_limit_bytes=24 * 2**20),
        name="subtract",
    )(*given)


def local(panel_cols, window_cols):
    return subtract(*gather_and_factor(panel_cols, window_cols))


def solution(mesh):
    return jax.shard_map(
        local,
        mesh=mesh,
        in_specs=(P("col", "row"), P("col", "row")),
        out_specs=(P(), P(("col", "row"), None), P("col", "row")),
        check_vma=False,
    )
```

```python
import jax
import jax.numpy as jnp
from jax import lax
from jax.experimental import pallas as pl
from jax.experimental.pallas import tpu as pltpu
from jax.sharding import PartitionSpec as P

MESH = pl.DeviceIdType.MESH
HIGHEST = lax.Precision.HIGHEST
F32 = jnp.float32
BF16 = jnp.bfloat16

N = 256
SLAB = 2048
DEPTH = 1024
PIECE = 32
HALF = 128
CHUNKS = 2
S1 = 256 // CHUNKS
S2 = S1 // 4
BLOCK = 64
TILES = 8


def dot_nt(a, b, precision=None):
    return lax.dot_general(a, b, (((1,), (1,)), ((), ())), precision=precision, preferred_element_type=F32)


def dot_nn(a, b, precision=None):
    return lax.dot_general(a, b, (((1,), (0,)), ((), ())), precision=precision, preferred_element_type=F32)


def dot_tn(a, b, precision=None):
    return lax.dot_general(a, b, (((0,), (0,)), ((), ())), precision=precision, preferred_element_type=F32)


def split(v):
    high = v.astype(BF16)
    return high, (v - high.astype(F32)).astype(BF16)


def spread_row(v, r):
    return jnp.broadcast_to(v[r:r + 1, :], (8, 128))


def spread_lane(v, c):
    return jnp.broadcast_to(v[:, c:c + 1], (8, 128))


def eliminate(groups, g):
    sub = lax.broadcasted_iota(jnp.int32, (8, 128), 0)
    v = groups[g]
    c = [spread_lane(v, 8 * g + t) for t in range(8)]
    w, m = [None] * 8, {}
    for t in range(0, 8, 2):
        r0, r1 = spread_row(v, t), spread_row(v, t + 1)
        p, q, r = spread_row(c[t], t), spread_row(c[t + 1], t), spread_row(c[t + 1], t + 1)
        over = 1.0 / (p * r - q * q)
        po, qo, ro = p * over, q * over, r * over
        w[t], w[t + 1] = ro * r0 - qo * r1, po * r1 - qo * r0
        for u in range(t + 2, 8):
            pu, su = spread_row(c[u], t), spread_row(c[u], t + 1)
            m[t, u], m[t + 1, u] = ro * pu - qo * su, po * su - qo * pu
            c[u] = c[u] - (c[t] * m[t, u] + c[t + 1] * m[t + 1, u])
        new = v - (c[t] * w[t] + c[t + 1] * w[t + 1])
        v = jnp.where(sub > t + 1, new, jnp.where(sub == t + 1, r1 - (q / p) * r0, v))
    groups[g] = v
    if g + 1 == len(groups):
        return
    solved = list(w)
    for t in (4, 2, 0):
        for s in (t, t + 1):
            total = m[s, t + 2] * solved[t + 2]
            for u in range(t + 3, 8):
                total = total + m[s, u] * solved[u]
            solved[s] = w[s] - total
    for i in range(g + 1, len(groups)):
        p = [spread_lane(groups[i], 8 * g + t) * solved[t] for t in range(8)]
        groups[i] = groups[i] - (((p[0] + p[1]) + (p[2] + p[3])) + ((p[4] + p[5]) + (p[6] + p[7])))


N_PANEL = 13
N_GRAM = 19
N_CROSS = 4 * CHUNKS * 24


def body(
    panel_hbm, w_hbm,
    u_out, inv_out, w_ref, f_ref, bh_out, bl_out,
    panel_ref, wh_ref, wl_ref, a_ref, ab_ref, g1_ref, g2_ref, gz_ref, t_ref,
    c_ref, r1_ref, r2_ref, w_sem, send_sem, recv_sem,
):
    row = lax.axis_index("row")
    col = lax.axis_index("col")
    y, x = lax.div(row, 4), lax.rem(row, 4)
    z, k = lax.div(col, 2), lax.rem(col, 2)

    def step(v, d):
        return lax.rem(v + d, 4)

    def at_x(d):
        return (y * 4 + step(x, d), col)

    def at_y(d):
        return (step(y, d) * 4 + x, col)

    def piece(d, core):
        return step(z, d) * 2 + core

    def at_z(d):
        return (row, piece(d, k))

    partner = (row, z * 2 + 1 - k)

    def load_window(b):
        where = pl.ds(b * 256, 256)
        return pltpu.make_async_copy(w_hbm.at[where, :], w_ref.at[where, :], w_sem.at[b])

    load_panel = pltpu.make_async_copy(panel_hbm, panel_ref, w_sem.at[8])
    load_panel.start()
    for b in range(8):
        load_window(b).start()

    barrier = pltpu.get_barrier_semaphore()
    others = [at_x(d) for d in (1, 2, 3)] + [at_y(d) for d in (1, 2, 3)] + [at_z(d) for d in (1, 2, 3)] + [partner]
    for dev in others:
        pl.semaphore_signal(barrier, inc=1, device_id=dev, device_id_type=MESH)
    load_panel.wait()
    pl.semaphore_wait(barrier, len(others))

    sent = []

    def send(index, src, dst, dev):
        copy = pltpu.make_async_remote_copy(
            src_ref=src, dst_ref=dst, send_sem=send_sem.at[index], recv_sem=recv_sem.at[index],
            device_id=dev, device_id_type=MESH,
        )
        copy.start()
        sent.append(copy)
        return copy

    half = (pl.ds(0, 16), pl.ds(16, 16))
    up, down = at_z(1), at_z(3)
    own = {}
    own["up0"] = send(0, panel_ref.at[half[0]], a_ref.at[col, half[0]], up)
    own["down1"] = send(1, panel_ref.at[half[1]], a_ref.at[col, half[1]], down)
    own["up1"] = send(2, panel_ref.at[half[1]], a_ref.at[col, half[1]], up)
    own["down0"] = send(3, panel_ref.at[half[0]], a_ref.at[col, half[0]], down)
    own["partner"] = send(4, panel_ref, a_ref.at[col], partner)
    a_ref[col] = panel_ref[...]

    def split_window(first, last):
        for b in range(first, last):
            rows = pl.ds(b * 256, 256)
            load_window(b).wait()
            high, low = split(w_ref[rows, :])
            wh_ref[rows, :] = high
            wl_ref[rows, :] = low

    below, above, far = piece(3, k), piece(1, k), piece(2, k)
    gram_blocks = [None] * 4

    def pass_on(index, who, h, dev):
        return send(index, a_ref.at[who, half[h]], a_ref.at[who, half[h]], dev)

    def pair_here(d):
        pair = a_ref[pl.ds(step(z, d) * 2, 2)].reshape(2 * PIECE, DEPTH)
        high, low = split(pair)
        ab_ref[d // 2, pl.ds(d % 2 * 64, 64), :] = high
        ab_ref[d // 2, pl.ds(HALF + d % 2 * 64, 64), :] = low
        gram_blocks[d] = dot_nt(panel_ref[...], pair, HIGHEST)

    split_window(0, 5)
    own["down1"].wait_recv()
    relay1 = pass_on(6, above, 1, down)
    forward_above = [pass_on(8, above, 1, partner)]
    own["up0"].wait_recv()
    relay0 = pass_on(5, below, 0, up)
    forward_below = [pass_on(7, below, 0, partner)]
    split_window(5, 8)
    own["partner"].wait_recv()
    pair_here(0)
    own["down0"].wait_recv()
    forward_above.append(pass_on(10, above, 0, partner))
    own["up1"].wait_recv()
    forward_below.append(pass_on(9, below, 1, partner))
    for copy in forward_above:
        copy.wait_recv()
    pair_here(1)

    def gram_start():
        slab = pltpu.roll(jnp.concatenate(gram_blocks, axis=1), z * 2 * PIECE, 1)
        copies = []
        for part, (me, at) in enumerate(((x, at_x), (y, at_y))):
            g1_ref[part, me] = slab[part * 16:part * 16 + 16, :]
            copies += [
                send(N_PANEL + part * 3 + d - 1, g1_ref.at[part, me], g1_ref.at[part, me], at(d)) for d in (1, 2, 3)
            ]
        return copies

    def summed(ref, part):
        return (ref[part, 0] + ref[part, 1]) + (ref[part, 2] + ref[part, 3])

    def gram_turn(arriving):
        copies = []
        for part, (me, at) in enumerate(((y, at_y), (x, at_x))):
            for copy in arriving[part * 3:part * 3 + 3]:
                copy.wait_recv()
            g2_ref[part, me] = summed(g1_ref, part)
            copies += [
                send(N_PANEL + 6 + part * 3 + d - 1, g2_ref.at[part, me], g2_ref.at[part, me], at(d)) for d in (1, 2, 3)
            ]
        return copies

    def gram_to_col(arriving):
        for part in range(2):
            for copy in arriving[part * 3:part * 3 + 3]:
                copy.wait_recv()
            gz_ref[col, part * 16:part * 16 + 16] = summed(g2_ref, part)
        copies = [send(N_PANEL + 12 + d - 1, gz_ref.at[col], gz_ref.at[col], at_z(d)) for d in (1, 3, 2)]
        return copies + [send(N_PANEL + 15, gz_ref.at[col], gz_ref.at[col], partner)]

    def gram_done(arriving):
        forwards = []
        for n, d in enumerate((3, 1, 2)):
            arriving[n].wait_recv()
            there = gz_ref.at[piece(d, k)]
            forwards.append(send(N_PANEL + 16 + n, there, there, partner))
        arriving[3].wait_recv()
        for copy in forwards:
            copy.wait_recv()
        t_ref[:, :N] = gz_ref[...].reshape(N, N)
        rows_at = lax.broadcasted_iota(jnp.int32, (N, N), 0)
        cols_at = lax.broadcasted_iota(jnp.int32, (N, N), 1)
        t_ref[:, N:] = jnp.where(rows_at == cols_at, 1.0, 0.0).astype(F32)

    sub = lax.broadcasted_iota(jnp.int32, (BLOCK, 128), 0)
    lane = lax.broadcasted_iota(jnp.int32, (BLOCK, 128), 1)
    groups = []

    def tile_of(lo, at):
        e = t_ref[lo:lo + BLOCK, at // 128 * 128:at // 128 * 128 + 128]
        return pltpu.roll(e, 128 - at % 128, 1) if at % 128 else e

    def begin(e):
        e = jnp.where(lane < BLOCK, e, jnp.where(lane == sub + BLOCK, 1.0, 0.0).astype(F32))
        groups[:] = [e[8 * i:8 * i + 8, :] for i in range(BLOCK // 8)]

    def apply(b):
        lo, hi = b * BLOCK, b * BLOCK + BLOCK
        e = jnp.concatenate(groups, axis=0)
        diagonal = jnp.sum(jnp.where(lane == sub, e, 0.0), axis=1, keepdims=True)
        root = lax.rsqrt(diagonal)
        root = root * (1.5 - 0.5 * diagonal * root * root)
        inverse = (e * root)[:, BLOCK:2 * BLOCK]
        if hi < N:
            ahead = dot_nn(inverse, tile_of(lo, hi), HIGHEST)
            begin(tile_of(hi, hi) - dot_tn(ahead[:, :BLOCK], ahead, HIGHEST))
        done = dot_nn(inverse, t_ref[lo:lo + BLOCK, :], HIGHEST)
        t_ref[lo:lo + BLOCK, :] = done
        if hi < N:
            update = dot_tn(done[:, :N], done, HIGHEST)
            t_ref[hi:, :] -= update[hi:, :]

    def finish():
        rows_at = lax.broadcasted_iota(jnp.int32, (N, N), 0)
        cols_at = lax.broadcasted_iota(jnp.int32, (N, N), 1)
        u_out[...] = jnp.where(cols_at >= rows_at, t_ref[:, :N], 0.0)
        inverse = jnp.where(cols_at <= rows_at, t_ref[:, N:], 0.0)
        inverse = pltpu.roll(inverse, lax.rem(4 - z, 4) * 2 * PIECE, 1)
        inv_out[...] = inverse
        ih, il = split(inverse)
        ah = jnp.concatenate([ab_ref[0, :HALF, :], ab_ref[1, :HALF, :]], axis=0)
        al = jnp.concatenate([ab_ref[0, HALF:, :], ab_ref[1, HALF:, :]], axis=0)
        qh, ql = split((dot_nn(ih, al) + dot_nn(il, ah)) + dot_nn(ih, ah))
        high, low = split((dot_tn(ih, ql) + dot_tn(il, qh)) + dot_tn(ih, qh))
        bh_out[...] = high
        bl_out[...] = low

    def pieces():
        begin(tile_of(0, 0))
        for b in range(N // BLOCK):
            for g in range(BLOCK // 8):
                eliminate(groups, g)
                if g in (1, 3, 5):
                    yield
            apply(b)

    def rows_of(start, size, align):
        return pl.ds(pl.multiple_of(start, align), size)

    def product(h, d):
        for part in range(2):
            where = rows_of(part * 1024 + step(y if part else x, d) * 256, 256, 256)
            both = dot_nt(wh_ref[where, :], ab_ref[h])
            low = dot_nt(wl_ref[where, :], ab_ref[h, :HALF, :])
            c_ref[h, where, :] = (both[:, HALF:] + low) + both[:, :HALF]

    class Stream:
        def __init__(self, h, chunk, part):
            self.h = h
            self.at = (at_y, at_x) if part else (at_x, at_y)
            self.me = (y, x) if part else (x, y)
            self.start = part * 1024 + chunk * S1
            number = (h * CHUNKS + chunk) * 2 + part
            self.index = N_PANEL + N_GRAM + number * 24
            self.buf = (r1_ref.at[number], r2_ref.at[number])

        def place(self, axis, d, h):
            size = S2 if axis else S1
            if axis:
                start = self.start + self.me[0] * 256 + step(self.me[1], d) * S2
            else:
                start = self.start + step(self.me[0], d) * 256
            return rows_of(start + h * (size // 2), size // 2, size // 2)

        def rs_send(self, axis, slot, src, d):
            return send(self.index + axis * 6 + slot, c_ref.at[self.h, src, :], self.buf[axis].at[slot], self.at[axis](d))

        def far_out(self, axis):
            self.rs = [None] * 6
            self.rs[0] = self.rs_send(axis, 0, self.place(axis, 2, 0), 1)
            self.rs[1] = self.rs_send(axis, 1, self.place(axis, 2, 1), 3)

        def near_out(self, axis):
            self.rs[2] = self.rs_send(axis, 2, self.place(axis, 1, 1), 1)
            self.rs[3] = self.rs_send(axis, 3, self.place(axis, 3, 0), 3)

        def relay(self, axis):
            for slot, (d, h) in enumerate(((1, 0), (3, 1))):
                self.rs[slot].wait_recv()
                where = self.place(axis, d, h)
                c_ref[self.h, where, :] += self.buf[axis][slot]
                self.rs[4 + slot] = self.rs_send(axis, 4 + slot, where, d)

        def gathered(self, axis, into):
            for slot in (2, 3, 4, 5):
                self.rs[slot].wait_recv()
            for h, (a, b) in enumerate(((3, 4), (2, 5))):
                where = self.place(axis, 0, h)
                into[self.h, where, :] = c_ref[self.h, where, :] + (self.buf[axis][a] + self.buf[axis][b])

        def ag_send(self, axis, slot, where, d):
            there = f_ref.at[self.h, where, :]
            return send(self.index + 12 + axis * 6 + slot, there, there, self.at[axis](d))

        def spread(self, axis):
            self.ag = [
                self.ag_send(axis, 0, self.place(axis, 0, 0), 1),
                self.ag_send(axis, 1, self.place(axis, 0, 1), 3),
                self.ag_send(axis, 2, self.place(axis, 0, 1), 1),
                self.ag_send(axis, 3, self.place(axis, 0, 0), 3),
            ]

        def hand_on(self, axis):
            self.ag[0].wait_recv()
            self.ag.append(self.ag_send(axis, 4, self.place(axis, 3, 0), 1))
            self.ag[1].wait_recv()
            self.ag.append(self.ag_send(axis, 5, self.place(axis, 1, 1), 3))

        def spread_done(self, axis):
            for slot in (2, 3, 4, 5):
                self.ag[slot].wait_recv()

    streams = [[Stream(h, chunk, part) for part in range(2)] for h in range(2) for chunk in range(CHUNKS)]

    def run(number, *which):
        for n in which:
            for s in streams[n]:
                if number == 0:
                    s.far_out(0)
                elif number == 1:
                    s.near_out(0)
                elif number == 2:
                    s.relay(0)
                elif number == 3:
                    s.gathered(0, c_ref)
                    s.far_out(1)
                    s.near_out(1)
                elif number == 4:
                    s.relay(1)
                elif number == 5:
                    s.gathered(1, f_ref)
                    s.spread(1)
                elif number == 6:
                    s.hand_on(1)
                elif number == 7:
                    s.spread_done(1)
                    s.spread(0)
                elif number == 8:
                    s.hand_on(0)
                elif number == 9:
                    s.spread_done(0)

    product(0, 2)
    run(0, 0, 1)
    product(0, 1)
    product(0, 3)
    for copy in forward_below:
        copy.wait_recv()
    pair_here(3)
    relay0.wait_recv()
    forward_far = [pass_on(11, far, 0, partner)]
    relay1.wait_recv()
    forward_far.append(pass_on(12, far, 1, partner))
    run(1, 0, 1)
    product(0, 0)
    for copy in forward_far:
        copy.wait_recv()
    pair_here(2)
    gram = gram_start()
    run(2, 0, 1)
    product(1, 2)
    run(0, 2, 3)
    gram = gram_turn(gram)
    run(3, 0, 1)
    product(1, 1)
    product(1, 3)
    run(1, 2, 3)
    gram = gram_to_col(gram)
    product(1, 0)
    run(2, 2, 3)
    run(4, 0, 1)
    run(3, 2, 3)
    run(5, 0, 1)
    gram_done(gram)
    work = pieces()
    plan = (
        (), ((6, 0, 1), (4, 2, 3)), ((7, 0, 1),), ((5, 2, 3),), ((8, 0, 1),), ((6, 2, 3),), ((9, 0, 1),),
        ((7, 2, 3),), (), ((8, 2, 3),), (), (),
    )
    for rounds in plan:
        for number, *which in rounds:
            run(number, *which)
        next(work, None)
    for _ in work:
        pass
    finish()
    run(9, 2, 3)

    for copy in sent:
        copy.wait_send()


def gather_and_factor(panel_cols, window_cols):
    vmem = pl.BlockSpec(memory_space=pltpu.VMEM)
    count = N_PANEL + N_GRAM + N_CROSS
    return pl.pallas_call(
        body,
        out_shape=(
            pltpu.VMEM((N, N), F32),
            pltpu.VMEM((N, N), F32),
            pltpu.VMEM((SLAB, DEPTH), F32),
            pltpu.VMEM((2, SLAB, HALF), F32),
            pltpu.VMEM((N, DEPTH), BF16),
            pltpu.VMEM((N, DEPTH), BF16),
        ),
        in_specs=[pl.BlockSpec(memory_space=pltpu.HBM)] * 2,
        out_specs=(vmem,) * 6,
        scratch_shapes=[
            pltpu.VMEM((PIECE, DEPTH), F32),
            pltpu.VMEM((SLAB, DEPTH), BF16),
            pltpu.VMEM((SLAB, DEPTH), BF16),
            pltpu.VMEM((8, PIECE, DEPTH), F32),
            pltpu.VMEM((2, 2 * HALF, DEPTH), BF16),
            pltpu.VMEM((2, 4, 16, N), F32),
            pltpu.VMEM((2, 4, 16, N), F32),
            pltpu.VMEM((8, PIECE, N), F32),
            pltpu.VMEM((N, 2 * N), F32),
            pltpu.VMEM((2, SLAB, HALF), F32),
            pltpu.VMEM((4 * CHUNKS, 6, S1 // 2, HALF), F32),
            pltpu.VMEM((4 * CHUNKS, 6, S2 // 2, HALF), F32),
            pltpu.SemaphoreType.DMA((9,)),
            pltpu.SemaphoreType.DMA((count,)),
            pltpu.SemaphoreType.DMA((count,)),
        ],
        compiler_params=pltpu.CompilerParams(
            collective_id=0, has_side_effects=True, vmem_limit_bytes=36 * 2**20
        ),
        name="gather_and_factor",
    )(panel_cols, window_cols)


def subtract_body(u_ref, inv_ref, w_ref, f_ref, bh_ref, bl_ref, u_out, top_out, out, r_ref, top_ref, sem):
    copies = [pltpu.make_async_copy(u_ref, u_out, sem.at[TILES])]
    copies[0].start()
    rows = SLAB // TILES
    for b in range(TILES):
        where = pl.ds(b * rows, rows)
        fh, fl = split(jnp.concatenate([f_ref[0, where, :], f_ref[1, where, :]], axis=1))
        bh = bh_ref[...]
        r_ref[where, :] = w_ref[where, :] - ((dot_nn(fh, bl_ref[...]) + dot_nn(fl, bh)) + dot_nn(fh, bh))
        copies.append(pltpu.make_async_copy(r_ref.at[where, :], out.at[where, :], sem.at[b]))
        copies[-1].start()
        if b == TILES - 2:
            mine = pl.ds(pl.multiple_of(lax.axis_index("row") * 128, 128), 128)
            share = jnp.concatenate([f_ref[0, mine, :], f_ref[1, mine, :]], axis=1)
            top_ref[...] = dot_nt(share, inv_ref[...], HIGHEST)
            copies.append(pltpu.make_async_copy(top_ref, top_out, sem.at[TILES + 1]))
            copies[-1].start()
    for copy in copies:
        copy.wait()


def subtract(*given):
    vmem = pl.BlockSpec(memory_space=pltpu.VMEM)
    anywhere = pl.BlockSpec(memory_space=pl.ANY)
    return pl.pallas_call(
        subtract_body,
        out_shape=(
            jax.ShapeDtypeStruct((N, N), F32),
            jax.ShapeDtypeStruct((128, N), F32),
            jax.ShapeDtypeStruct((SLAB, DEPTH), F32),
        ),
        in_specs=[vmem] * 6,
        out_specs=(anywhere,) * 3,
        scratch_shapes=[
            pltpu.VMEM((SLAB, DEPTH), F32),
            pltpu.VMEM((128, N), F32),
            pltpu.SemaphoreType.DMA((TILES + 2,)),
        ],
        compiler_params=pltpu.CompilerParams(vmem_limit_bytes=24 * 2**20),
        name="subtract",
    )(*given)


def local(panel_cols, window_cols):
    return subtract(*gather_and_factor(panel_cols, window_cols))


def solution(mesh):
    return jax.shard_map(
        local,
        mesh=mesh,
        in_specs=(P("col", "row"), P("col", "row")),
        out_specs=(P(), P(("col", "row"), None), P("col", "row")),
        check_vma=False,
    )
```

```python
import jax
import jax.numpy as jnp
from jax import lax
from jax.experimental import pallas as pl
from jax.experimental.pallas import tpu as pltpu
from jax.sharding import PartitionSpec as P

MESH = pl.DeviceIdType.MESH
HIGHEST = lax.Precision.HIGHEST
F32 = jnp.float32
BF16 = jnp.bfloat16

N = 256
SLAB = 2048
DEPTH = 1024
PIECE = 32
HALF = 128
CHUNKS = 1
S1 = 256 // CHUNKS
S2 = S1 // 4
BLOCK = 64
TILES = 8


ORDER = (
    0, 1, 2, 3, 4, 5, 6, 14, 7, 9, 8, 11, 10, 17, 15, 12, 13, 46, 58, 47, 68, 43, 44, 48, 16, 18, 59, 55, 88, 45, 49,
    69, 52, 60, 61, 42, 50, 53, 54, 78, 71, 19, 70, 56, 90, 79, 51, 57, 91, 89, 62, 80, 81, 20, 72, 92, 82, 21, 22,
    63, 23, 73, 24, 26, 93, 83, 27, 28, 64, 74, 29, 30, 31, 94, 84, 32, 33, 75, 65, 66, 76, 34, 35, 36, 37, 85, 86,
    95, 96, 38, 39, 40, 41, 25, 67, 77, 87, 97,
)


def dot_nt(a, b, precision=None):
    return lax.dot_general(a, b, (((1,), (1,)), ((), ())), precision=precision, preferred_element_type=F32)


def dot_nn(a, b, precision=None):
    return lax.dot_general(a, b, (((1,), (0,)), ((), ())), precision=precision, preferred_element_type=F32)


def dot_tn(a, b, precision=None):
    return lax.dot_general(a, b, (((0,), (0,)), ((), ())), precision=precision, preferred_element_type=F32)


def split(v):
    high = v.astype(BF16)
    return high, (v - high.astype(F32)).astype(BF16)


def spread_row(v, r):
    return jnp.broadcast_to(v[r:r + 1, :], (8, 128))


def spread_lane(v, c):
    return jnp.broadcast_to(v[:, c:c + 1], (8, 128))


def eliminate(groups, g):
    sub = lax.broadcasted_iota(jnp.int32, (8, 128), 0)
    v = groups[g]
    c = [spread_lane(v, 8 * g + t) for t in range(8)]
    w, m = [None] * 8, {}
    for t in range(0, 8, 2):
        r0, r1 = spread_row(v, t), spread_row(v, t + 1)
        p, q, r = spread_row(c[t], t), spread_row(c[t + 1], t), spread_row(c[t + 1], t + 1)
        over = 1.0 / (p * r - q * q)
        po, qo, ro = p * over, q * over, r * over
        w[t], w[t + 1] = ro * r0 - qo * r1, po * r1 - qo * r0
        for u in range(t + 2, 8):
            pu, su = spread_row(c[u], t), spread_row(c[u], t + 1)
            m[t, u], m[t + 1, u] = ro * pu - qo * su, po * su - qo * pu
            c[u] = c[u] - (c[t] * m[t, u] + c[t + 1] * m[t + 1, u])
        new = v - (c[t] * w[t] + c[t + 1] * w[t + 1])
        v = jnp.where(sub > t + 1, new, jnp.where(sub == t + 1, r1 - (q / p) * r0, v))
    groups[g] = v
    if g + 1 == len(groups):
        return
    solved = list(w)
    for t in (4, 2, 0):
        for s in (t, t + 1):
            total = m[s, t + 2] * solved[t + 2]
            for u in range(t + 3, 8):
                total = total + m[s, u] * solved[u]
            solved[s] = w[s] - total
    for i in range(g + 1, len(groups)):
        p = [spread_lane(groups[i], 8 * g + t) * solved[t] for t in range(8)]
        groups[i] = groups[i] - (((p[0] + p[1]) + (p[2] + p[3])) + ((p[4] + p[5]) + (p[6] + p[7])))


N_PANEL = 13
N_GRAM = 19
N_CROSS = 4 * CHUNKS * 18


def body(
    panel_hbm, w_hbm,
    u_out, ih_out, il_out, w_ref, f_ref, bh_out, bl_out,
    panel_ref, wh_ref, wl_ref, a_ref, ab_ref, g1_ref, g2_ref, gz_ref, t_ref,
    c_ref, r1_ref, r2_ref, w_sem, send_sem, recv_sem,
):
    row = lax.axis_index("row")
    col = lax.axis_index("col")
    y, x = lax.div(row, 4), lax.rem(row, 4)
    z, k = lax.div(col, 2), lax.rem(col, 2)

    def step(v, d):
        return lax.rem(v + d, 4)

    def at_x(d):
        return (y * 4 + step(x, d), col)

    def at_y(d):
        return (step(y, d) * 4 + x, col)

    def piece(d, core):
        return step(z, d) * 2 + core

    def at_z(d):
        return (row, piece(d, k))

    partner = (row, z * 2 + 1 - k)

    def load_window(b):
        where = pl.ds(b * 256, 256)
        return pltpu.make_async_copy(w_hbm.at[where, :], w_ref.at[where, :], w_sem.at[b])

    load_panel = pltpu.make_async_copy(panel_hbm, panel_ref, w_sem.at[8])
    load_panel.start()
    for b in range(8):
        load_window(b).start()

    barrier = pltpu.get_barrier_semaphore()
    others = [at_x(d) for d in (1, 2, 3)] + [at_y(d) for d in (1, 2, 3)] + [at_z(d) for d in (1, 2, 3)] + [partner]
    for dev in others:
        pl.semaphore_signal(barrier, inc=1, device_id=dev, device_id_type=MESH)
    load_panel.wait()
    pl.semaphore_wait(barrier, len(others))

    sent = []

    def send(index, src, dst, dev):
        copy = pltpu.make_async_remote_copy(
            src_ref=src, dst_ref=dst, send_sem=send_sem.at[index], recv_sem=recv_sem.at[index],
            device_id=dev, device_id_type=MESH,
        )
        copy.start()
        sent.append(copy)
        return copy

    half = (pl.ds(0, 16), pl.ds(16, 16))
    up, down = at_z(1), at_z(3)
    own = {}
    own["up0"] = send(0, panel_ref.at[half[0]], a_ref.at[col, half[0]], up)
    own["down1"] = send(1, panel_ref.at[half[1]], a_ref.at[col, half[1]], down)
    own["up1"] = send(2, panel_ref.at[half[1]], a_ref.at[col, half[1]], up)
    own["down0"] = send(3, panel_ref.at[half[0]], a_ref.at[col, half[0]], down)
    own["partner"] = send(4, panel_ref, a_ref.at[col], partner)
    a_ref[col] = panel_ref[...]

    ops = []

    def split_window(b):
        rows = pl.ds(b * 256, 256)
        load_window(b).wait()
        high, low = split(w_ref[rows, :])
        wh_ref[rows, :] = high
        wl_ref[rows, :] = low

    for b in range(8):
        ops.append(lambda b=b: split_window(b))

    below, above, far = piece(3, k), piece(1, k), piece(2, k)
    gram_blocks = [None] * 4
    passed = {}

    def pass_on(index, who, h, dev):
        return send(index, a_ref.at[who, half[h]], a_ref.at[who, half[h]], dev)

    def pair_here(d, *needs):
        for copy in needs:
            copy.wait_recv()
        pair = a_ref[pl.ds(step(z, d) * 2, 2)].reshape(2 * PIECE, DEPTH)
        high, low = split(pair)
        ab_ref[d // 2, pl.ds(d % 2 * 64, 64), :] = high
        ab_ref[d // 2, pl.ds(HALF + d % 2 * 64, 64), :] = low
        gram_blocks[d] = dot_nt(panel_ref[...], pair, HIGHEST)

    @ops.append
    def _():
        own["down1"].wait_recv()
        passed["relay1"] = pass_on(6, above, 1, down)
        passed["above1"] = pass_on(8, above, 1, partner)

    @ops.append
    def _():
        own["up0"].wait_recv()
        passed["relay0"] = pass_on(5, below, 0, up)
        passed["below0"] = pass_on(7, below, 0, partner)

    @ops.append
    def _():
        own["down0"].wait_recv()
        passed["above0"] = pass_on(10, above, 0, partner)

    @ops.append
    def _():
        own["up1"].wait_recv()
        passed["below1"] = pass_on(9, below, 1, partner)

    @ops.append
    def _():
        passed["relay0"].wait_recv()
        passed["far0"] = pass_on(11, far, 0, partner)

    @ops.append
    def _():
        passed["relay1"].wait_recv()
        passed["far1"] = pass_on(12, far, 1, partner)

    ops.append(lambda: pair_here(0, own["partner"]))
    ops.append(lambda: pair_here(1, passed["above0"], passed["above1"]))
    ops.append(lambda: pair_here(2, passed["far0"], passed["far1"]))
    ops.append(lambda: pair_here(3, passed["below0"], passed["below1"]))

    gram = {}

    @ops.append
    def _():
        slab = pltpu.roll(jnp.concatenate(gram_blocks, axis=1), z * 2 * PIECE, 1)
        gram["first"] = []
        for part, (me, at) in enumerate(((x, at_x), (y, at_y))):
            g1_ref[part, me] = slab[part * 16:part * 16 + 16, :]
            gram["first"] += [
                send(N_PANEL + part * 3 + d - 1, g1_ref.at[part, me], g1_ref.at[part, me], at(d)) for d in (1, 2, 3)
            ]

    def summed(ref, part):
        return (ref[part, 0] + ref[part, 1]) + (ref[part, 2] + ref[part, 3])

    @ops.append
    def _():
        gram["second"] = []
        for part, (me, at) in enumerate(((y, at_y), (x, at_x))):
            for copy in gram["first"][part * 3:part * 3 + 3]:
                copy.wait_recv()
            g2_ref[part, me] = summed(g1_ref, part)
            gram["second"] += [
                send(N_PANEL + 6 + part * 3 + d - 1, g2_ref.at[part, me], g2_ref.at[part, me], at(d)) for d in (1, 2, 3)
            ]

    @ops.append
    def _():
        for part in range(2):
            for copy in gram["second"][part * 3:part * 3 + 3]:
                copy.wait_recv()
            gz_ref[col, part * 16:part * 16 + 16] = summed(g2_ref, part)
        gram["col"] = {d: send(N_PANEL + 12 + d - 1, gz_ref.at[col], gz_ref.at[col], at_z(d)) for d in (1, 3, 2)}
        gram["partner"] = [send(N_PANEL + 15, gz_ref.at[col], gz_ref.at[col], partner)]

    def gram_forward(d):
        gram["col"][d].wait_recv()
        there = gz_ref.at[piece(4 - d, k)]
        gram["partner"].append(send(N_PANEL + 15 + d, there, there, partner))

    for d in (1, 3, 2):
        ops.append(lambda d=d: gram_forward(d))

    @ops.append
    def _():
        for copy in gram["partner"]:
            copy.wait_recv()
        t_ref[:, :N] = gz_ref[...].reshape(N, N)
        rows_at = lax.broadcasted_iota(jnp.int32, (N, N), 0)
        cols_at = lax.broadcasted_iota(jnp.int32, (N, N), 1)
        t_ref[:, N:] = jnp.where(rows_at == cols_at, 1.0, 0.0).astype(F32)

    sub = lax.broadcasted_iota(jnp.int32, (BLOCK, 128), 0)
    lane = lax.broadcasted_iota(jnp.int32, (BLOCK, 128), 1)
    groups = []

    def tile_of(lo, at):
        e = t_ref[lo:lo + BLOCK, at // 128 * 128:at // 128 * 128 + 128]
        return pltpu.roll(e, 128 - at % 128, 1) if at % 128 else e

    def begin(e):
        e = jnp.where(lane < BLOCK, e, jnp.where(lane == sub + BLOCK, 1.0, 0.0).astype(F32))
        groups[:] = [e[8 * i:8 * i + 8, :] for i in range(BLOCK // 8)]

    def apply(b):
        lo, hi = b * BLOCK, b * BLOCK + BLOCK
        e = jnp.concatenate(groups, axis=0)
        diagonal = jnp.sum(jnp.where(lane == sub, e, 0.0), axis=1, keepdims=True)
        root = lax.rsqrt(diagonal)
        root = root * (1.5 - 0.5 * diagonal * root * root)
        inverse = (e * root)[:, BLOCK:2 * BLOCK]
        if hi < N:
            ahead = dot_nn(inverse, tile_of(lo, hi), HIGHEST)
            begin(tile_of(hi, hi) - dot_tn(ahead[:, :BLOCK], ahead, HIGHEST))
        done = dot_nn(inverse, t_ref[lo:lo + BLOCK, :], HIGHEST)
        t_ref[lo:lo + BLOCK, :] = done
        if hi < N:
            update = dot_tn(done[:, :N], done, HIGHEST)
            t_ref[hi:, :] -= update[hi:, :]

    @ops.append
    def _():
        rows_at = lax.broadcasted_iota(jnp.int32, (N, N), 0)
        cols_at = lax.broadcasted_iota(jnp.int32, (N, N), 1)
        u_out[...] = jnp.where(cols_at >= rows_at, t_ref[:, :N], 0.0)
        inverse = jnp.where(cols_at <= rows_at, t_ref[:, N:], 0.0)
        inverse = pltpu.roll(inverse, lax.rem(4 - z, 4) * 2 * PIECE, 1)
        ih, il = split(inverse)
        ih_out[...] = ih
        il_out[...] = il
        ah = jnp.concatenate([ab_ref[0, :HALF, :], ab_ref[1, :HALF, :]], axis=0)
        al = jnp.concatenate([ab_ref[0, HALF:, :], ab_ref[1, HALF:, :]], axis=0)
        qh, ql = split((dot_nn(ih, al) + dot_nn(il, ah)) + dot_nn(ih, ah))
        high, low = split((dot_tn(ih, ql) + dot_tn(il, qh)) + dot_tn(ih, qh))
        bh_out[...] = high
        bl_out[...] = low

    def pieces():
        begin(tile_of(0, 0))
        for b in range(N // BLOCK):
            for g in range(BLOCK // 8):
                eliminate(groups, g)
                if g in (1, 3, 5):
                    yield
                if g == 7:
                    apply(b)
                    yield

    work = pieces()
    for n in range(4 * N // BLOCK):
        ops.append(lambda: next(work))

    def rows_of(start, size, align):
        return pl.ds(pl.multiple_of(start, align), size)

    def product(h, d, part):
        where = rows_of(part * 1024 + step(y if part else x, d) * 256, 256, 256)
        both = dot_nt(wh_ref[where, :], ab_ref[h])
        low = dot_nt(wl_ref[where, :], ab_ref[h, :HALF, :])
        c_ref[h, where, :] = (both[:, HALF:] + low) + both[:, :HALF]

    for h in range(2):
        for d in range(4):
            for part in range(2):
                ops.append(lambda h=h, d=d, part=part: product(h, d, part))

    class Stream:
        def __init__(self, h, chunk, part):
            self.h = h
            self.at = (at_y, at_x) if part else (at_x, at_y)
            self.me = (y, x) if part else (x, y)
            self.start = part * 1024 + chunk * S1
            self.number = (h * CHUNKS + chunk) * 2 + part
            self.index = N_PANEL + N_GRAM + self.number * 18
            self.first, self.second, self.back, self.last = {}, {}, {}, {}

        def near(self, d, h):
            start = self.start + step(self.me[0], d) * 256
            return rows_of(start + h * (S1 // 2), S1 // 2, S1 // 2)

        def share(self, d):
            return rows_of(self.start + self.me[0] * 256 + step(self.me[1], d) * S2, S2, S2)

        def sum_out(self, slot, where, d):
            there = r1_ref.at[self.number, slot]
            self.first[slot] = send(self.index + slot, c_ref.at[self.h, where, :], there, self.at[0](d))

        def far_out(self):
            self.sum_out(0, self.near(2, 0), 1)
            self.sum_out(1, self.near(2, 1), 3)

        def near_out(self):
            self.sum_out(2, self.near(1, 1), 1)
            self.sum_out(3, self.near(3, 0), 3)

        def relay(self, slot):
            d = (1, 3)[slot]
            self.first[slot].wait_recv()
            where = self.near(d, slot)
            c_ref[self.h, where, :] += r1_ref[self.number, slot]
            self.sum_out(4 + slot, where, d)

        def turn(self):
            for slot in (2, 3, 4, 5):
                self.first[slot].wait_recv()
            for h, (a, b) in enumerate(((3, 4), (2, 5))):
                where = self.near(0, h)
                c_ref[self.h, where, :] += r1_ref[self.number, a] + r1_ref[self.number, b]
            for d in (2, 1, 3):
                there = r2_ref.at[self.number, d - 1]
                src = c_ref.at[self.h, self.share(d), :]
                self.second[d] = send(self.index + 5 + d, src, there, self.at[1](d))

        def complete(self):
            for d in (1, 2, 3):
                self.second[d].wait_recv()
            where = self.share(0)
            mine = c_ref[self.h, where, :] + r2_ref[self.number, 0]
            f_ref[self.h, where, :] = mine + (r2_ref[self.number, 1] + r2_ref[self.number, 2])
            there = f_ref.at[self.h, where, :]
            for d in (2, 1, 3):
                self.back[d] = send(self.index + 8 + d, there, there, self.at[1](d))

        def spread_out(self, slot, d, h, to):
            there = f_ref.at[self.h, self.near(d, h), :]
            self.last[slot] = send(self.index + 12 + slot, there, there, self.at[0](to))

        def spread(self):
            for d in (1, 2, 3):
                self.back[d].wait_recv()
            self.spread_out(0, 0, 0, 1)
            self.spread_out(1, 0, 1, 3)
            self.spread_out(2, 0, 1, 1)
            self.spread_out(3, 0, 0, 3)

        def hand_on(self, slot):
            self.last[slot].wait_recv()
            self.spread_out(4 + slot, (3, 1)[slot], slot, (1, 3)[slot])

        def end(self):
            for slot in (2, 3, 4, 5):
                self.last[slot].wait_recv()

    for h in range(2):
        for chunk in range(CHUNKS):
            for part in range(2):
                s = Stream(h, chunk, part)
                ops += [s.far_out, s.near_out, lambda s=s: s.relay(0), lambda s=s: s.relay(1), s.turn]
                ops += [s.complete, s.spread, lambda s=s: s.hand_on(0), lambda s=s: s.hand_on(1), s.end]

    assert sorted(ORDER) == list(range(len(ops)))
    for n in ORDER:
        ops[n]()
    for copy in sent:
        copy.wait_send()


def gather_and_factor(panel_cols, window_cols):
    vmem = pl.BlockSpec(memory_space=pltpu.VMEM)
    count = N_PANEL + N_GRAM + N_CROSS
    return pl.pallas_call(
        body,
        out_shape=(
            pltpu.VMEM((N, N), F32),
            pltpu.VMEM((N, N), BF16),
            pltpu.VMEM((N, N), BF16),
            pltpu.VMEM((SLAB, DEPTH), F32),
            pltpu.VMEM((2, SLAB, HALF), F32),
            pltpu.VMEM((N, DEPTH), BF16),
            pltpu.VMEM((N, DEPTH), BF16),
        ),
        in_specs=[pl.BlockSpec(memory_space=pltpu.HBM)] * 2,
        out_specs=(vmem,) * 7,
        scratch_shapes=[
            pltpu.VMEM((PIECE, DEPTH), F32),
            pltpu.VMEM((SLAB, DEPTH), BF16),
            pltpu.VMEM((SLAB, DEPTH), BF16),
            pltpu.VMEM((8, PIECE, DEPTH), F32),
            pltpu.VMEM((2, 2 * HALF, DEPTH), BF16),
            pltpu.VMEM((2, 4, 16, N), F32),
            pltpu.VMEM((2, 4, 16, N), F32),
            pltpu.VMEM((8, PIECE, N), F32),
            pltpu.VMEM((N, 2 * N), F32),
            pltpu.VMEM((2, SLAB, HALF), F32),
            pltpu.VMEM((4 * CHUNKS, 6, S1 // 2, HALF), F32),
            pltpu.VMEM((4 * CHUNKS, 3, S2, HALF), F32),
            pltpu.SemaphoreType.DMA((9,)),
            pltpu.SemaphoreType.DMA((count,)),
            pltpu.SemaphoreType.DMA((count,)),
        ],
        compiler_params=pltpu.CompilerParams(
            collective_id=0, has_side_effects=True, vmem_limit_bytes=54900000
        ),
        name="gather_and_factor",
    )(panel_cols, window_cols)


def subtract_body(u_ref, ih_ref, il_ref, w_ref, f_ref, bh_ref, bl_ref, u_out, top_out, out, r_ref, top_ref, sem):
    copies = [pltpu.make_async_copy(u_ref, u_out, sem.at[TILES])]
    copies[0].start()
    rows = SLAB // TILES
    for b in range(TILES):
        where = pl.ds(b * rows, rows)
        fh, fl = split(jnp.concatenate([f_ref[0, where, :], f_ref[1, where, :]], axis=1))
        bh = bh_ref[...]
        r_ref[where, :] = w_ref[where, :] - ((dot_nn(fh, bl_ref[...]) + dot_nn(fl, bh)) + dot_nn(fh, bh))
        copies.append(pltpu.make_async_copy(r_ref.at[where, :], out.at[where, :], sem.at[b]))
        copies[-1].start()
        if b == TILES - 2:
            mine = pl.ds(pl.multiple_of(lax.axis_index("row") * 128, 128), 128)
            fh, fl = split(jnp.concatenate([f_ref[0, mine, :], f_ref[1, mine, :]], axis=1))
            ih = ih_ref[...]
            top_ref[...] = (dot_nt(fh, il_ref[...]) + dot_nt(fl, ih)) + dot_nt(fh, ih)
            copies.append(pltpu.make_async_copy(top_ref, top_out, sem.at[TILES + 1]))
            copies[-1].start()
    for copy in copies:
        copy.wait()


def subtract(*given):
    vmem = pl.BlockSpec(memory_space=pltpu.VMEM)
    anywhere = pl.BlockSpec(memory_space=pl.ANY)
    return pl.pallas_call(
        subtract_body,
        out_shape=(
            jax.ShapeDtypeStruct((N, N), F32),
            jax.ShapeDtypeStruct((128, N), F32),
            jax.ShapeDtypeStruct((SLAB, DEPTH), F32),
        ),
        in_specs=[vmem] * 7,
        out_specs=(anywhere,) * 3,
        scratch_shapes=[
            pltpu.VMEM((SLAB, DEPTH), F32),
            pltpu.VMEM((128, N), F32),
            pltpu.SemaphoreType.DMA((TILES + 2,)),
        ],
        compiler_params=pltpu.CompilerParams(vmem_limit_bytes=24 * 2**20),
        name="subtract",
    )(*given)


def local(panel_cols, window_cols):
    return subtract(*gather_and_factor(panel_cols, window_cols))


def solution(mesh):
    return jax.shard_map(
        local,
        mesh=mesh,
        in_specs=(P("col", "row"), P("col", "row")),
        out_specs=(P(), P(("col", "row"), None), P("col", "row")),
        check_vma=False,
    )
```

```python
import jax
import jax.numpy as jnp
from jax import lax
from jax.experimental import pallas as pl
from jax.experimental.pallas import tpu as pltpu
from jax.sharding import PartitionSpec as P

MESH = pl.DeviceIdType.MESH
HIGHEST = lax.Precision.HIGHEST
F32 = jnp.float32
BF16 = jnp.bfloat16

N = 256
SLAB = 2048
DEPTH = 1024
PIECE = 32
HALF = 128
CHUNKS = 1
S1 = 256 // CHUNKS
S2 = S1 // 4
BLOCK = 64
TILES = 8


ORDER = (
    0, 1, 2, 3, 4, 5, 6, 14, 7, 9, 8, 11, 10, 17, 15, 38, 50, 13, 12, 39, 60, 36, 40, 51, 37, 41, 61, 16, 18, 46, 70,
    47, 80, 44, 52, 53, 63, 62, 48, 71, 49, 45, 34, 35, 42, 43, 19, 81, 72, 73, 82, 83, 54, 64, 20, 74, 84, 65, 55,
    23, 21, 22, 75, 24, 85, 26, 56, 66, 27, 86, 76, 28, 29, 58, 67, 57, 68, 30, 77, 78, 87, 88, 31, 32, 33, 59, 69,
    79, 89, 25,
)


def dot_nt(a, b, precision=None):
    return lax.dot_general(a, b, (((1,), (1,)), ((), ())), precision=precision, preferred_element_type=F32)


def dot_nn(a, b, precision=None):
    return lax.dot_general(a, b, (((1,), (0,)), ((), ())), precision=precision, preferred_element_type=F32)


def dot_tn(a, b, precision=None):
    return lax.dot_general(a, b, (((0,), (0,)), ((), ())), precision=precision, preferred_element_type=F32)


def split(v):
    high = v.astype(BF16)
    return high, (v - high.astype(F32)).astype(BF16)


def spread_row(v, r):
    return jnp.broadcast_to(v[r:r + 1, :], (8, 128))


def spread_lane(v, c):
    return jnp.broadcast_to(v[:, c:c + 1], (8, 128))


def eliminate(groups, g):
    sub = lax.broadcasted_iota(jnp.int32, (8, 128), 0)
    v = groups[g]
    c = [spread_lane(v, 8 * g + t) for t in range(8)]
    w, m = [None] * 8, {}
    for t in range(0, 8, 2):
        r0, r1 = spread_row(v, t), spread_row(v, t + 1)
        p, q, r = spread_row(c[t], t), spread_row(c[t + 1], t), spread_row(c[t + 1], t + 1)
        over = 1.0 / (p * r - q * q)
        po, qo, ro = p * over, q * over, r * over
        w[t], w[t + 1] = ro * r0 - qo * r1, po * r1 - qo * r0
        for u in range(t + 2, 8):
            pu, su = spread_row(c[u], t), spread_row(c[u], t + 1)
            m[t, u], m[t + 1, u] = ro * pu - qo * su, po * su - qo * pu
            c[u] = c[u] - (c[t] * m[t, u] + c[t + 1] * m[t + 1, u])
        new = v - (c[t] * w[t] + c[t + 1] * w[t + 1])
        v = jnp.where(sub > t + 1, new, jnp.where(sub == t + 1, r1 - (q / p) * r0, v))
    groups[g] = v
    if g + 1 == len(groups):
        return
    solved = list(w)
    for t in (4, 2, 0):
        for s in (t, t + 1):
            total = m[s, t + 2] * solved[t + 2]
            for u in range(t + 3, 8):
                total = total + m[s, u] * solved[u]
            solved[s] = w[s] - total
    for i in range(g + 1, len(groups)):
        p = [spread_lane(groups[i], 8 * g + t) * solved[t] for t in range(8)]
        groups[i] = groups[i] - (((p[0] + p[1]) + (p[2] + p[3])) + ((p[4] + p[5]) + (p[6] + p[7])))


N_PANEL = 13
N_GRAM = 19
N_CROSS = 4 * CHUNKS * 18


def body(
    panel_hbm, w_hbm,
    u_out, ih_out, il_out, w_ref, f_ref, bh_out, bl_out,
    panel_ref, wh_ref, wl_ref, a_ref, ab_ref, g1_ref, g2_ref, gz_ref, t_ref,
    q_ref, c_ref, r1_ref, r2_ref, w_sem, send_sem, recv_sem,
):
    row = lax.axis_index("row")
    col = lax.axis_index("col")
    y, x = lax.div(row, 4), lax.rem(row, 4)
    z, k = lax.div(col, 2), lax.rem(col, 2)

    def step(v, d):
        return lax.rem(v + d, 4)

    def at_x(d):
        return (y * 4 + step(x, d), col)

    def at_y(d):
        return (step(y, d) * 4 + x, col)

    def piece(d, core):
        return step(z, d) * 2 + core

    def at_z(d):
        return (row, piece(d, k))

    partner = (row, z * 2 + 1 - k)

    def load_window(b):
        where = pl.ds(b * 256, 256)
        return pltpu.make_async_copy(w_hbm.at[where, :], w_ref.at[where, :], w_sem.at[b])

    load_panel = pltpu.make_async_copy(panel_hbm, panel_ref, w_sem.at[8])
    load_panel.start()
    for b in range(8):
        load_window(b).start()

    barrier = pltpu.get_barrier_semaphore()
    others = [at_x(d) for d in (1, 2, 3)] + [at_y(d) for d in (1, 2, 3)] + [at_z(d) for d in (1, 2, 3)] + [partner]
    for dev in others:
        pl.semaphore_signal(barrier, inc=1, device_id=dev, device_id_type=MESH)
    load_panel.wait()
    pl.semaphore_wait(barrier, len(others))

    sent = []

    def send(index, src, dst, dev):
        copy = pltpu.make_async_remote_copy(
            src_ref=src, dst_ref=dst, send_sem=send_sem.at[index], recv_sem=recv_sem.at[index],
            device_id=dev, device_id_type=MESH,
        )
        copy.start()
        sent.append(copy)
        return copy

    half = (pl.ds(0, 16), pl.ds(16, 16))
    up, down = at_z(1), at_z(3)
    own = {}
    own["up0"] = send(0, panel_ref.at[half[0]], a_ref.at[col, half[0]], up)
    own["down1"] = send(1, panel_ref.at[half[1]], a_ref.at[col, half[1]], down)
    own["up1"] = send(2, panel_ref.at[half[1]], a_ref.at[col, half[1]], up)
    own["down0"] = send(3, panel_ref.at[half[0]], a_ref.at[col, half[0]], down)
    own["partner"] = send(4, panel_ref, a_ref.at[col], partner)
    a_ref[col] = panel_ref[...]

    ops = []

    def split_window(b):
        rows = pl.ds(b * 256, 256)
        load_window(b).wait()
        high, low = split(w_ref[rows, :])
        wh_ref[rows, :] = high
        wl_ref[rows, :] = low

    for b in range(8):
        ops.append(lambda b=b: split_window(b))

    below, above, far = piece(3, k), piece(1, k), piece(2, k)
    gram_blocks = [None] * 4
    passed = {}

    def pass_on(index, who, h, dev):
        return send(index, a_ref.at[who, half[h]], a_ref.at[who, half[h]], dev)

    def pair_here(d, *needs):
        for copy in needs:
            copy.wait_recv()
        pair = a_ref[pl.ds(step(z, d) * 2, 2)].reshape(2 * PIECE, DEPTH)
        high, low = split(pair)
        ab_ref[d // 2, pl.ds(d % 2 * 64, 64), :] = high
        ab_ref[d // 2, pl.ds(HALF + d % 2 * 64, 64), :] = low
        gram_blocks[d] = dot_nt(panel_ref[...], pair, HIGHEST)

    @ops.append
    def _():
        own["down1"].wait_recv()
        passed["relay1"] = pass_on(6, above, 1, down)
        passed["above1"] = pass_on(8, above, 1, partner)

    @ops.append
    def _():
        own["up0"].wait_recv()
        passed["relay0"] = pass_on(5, below, 0, up)
        passed["below0"] = pass_on(7, below, 0, partner)

    @ops.append
    def _():
        own["down0"].wait_recv()
        passed["above0"] = pass_on(10, above, 0, partner)

    @ops.append
    def _():
        own["up1"].wait_recv()
        passed["below1"] = pass_on(9, below, 1, partner)

    @ops.append
    def _():
        passed["relay0"].wait_recv()
        passed["far0"] = pass_on(11, far, 0, partner)

    @ops.append
    def _():
        passed["relay1"].wait_recv()
        passed["far1"] = pass_on(12, far, 1, partner)

    ops.append(lambda: pair_here(0, own["partner"]))
    ops.append(lambda: pair_here(1, passed["above0"], passed["above1"]))
    ops.append(lambda: pair_here(2, passed["far0"], passed["far1"]))
    ops.append(lambda: pair_here(3, passed["below0"], passed["below1"]))

    gram = {}

    @ops.append
    def _():
        slab = pltpu.roll(jnp.concatenate(gram_blocks, axis=1), z * 2 * PIECE, 1)
        gram["first"] = []
        for part, (me, at) in enumerate(((x, at_x), (y, at_y))):
            g1_ref[part, me] = slab[part * 16:part * 16 + 16, :]
            gram["first"] += [
                send(N_PANEL + part * 3 + d - 1, g1_ref.at[part, me], g1_ref.at[part, me], at(d)) for d in (2, 1, 3)
            ]

    def summed(ref, part):
        return (ref[part, 0] + ref[part, 1]) + (ref[part, 2] + ref[part, 3])

    @ops.append
    def _():
        gram["second"] = []
        for part, (me, at) in enumerate(((y, at_y), (x, at_x))):
            for copy in gram["first"][part * 3:part * 3 + 3]:
                copy.wait_recv()
            g2_ref[part, me] = summed(g1_ref, part)
            gram["second"] += [
                send(N_PANEL + 6 + part * 3 + d - 1, g2_ref.at[part, me], g2_ref.at[part, me], at(d)) for d in (2, 1, 3)
            ]

    @ops.append
    def _():
        for part in range(2):
            for copy in gram["second"][part * 3:part * 3 + 3]:
                copy.wait_recv()
            gz_ref[col, part * 16:part * 16 + 16] = summed(g2_ref, part)
        gram["col"] = {d: send(N_PANEL + 12 + d - 1, gz_ref.at[col], gz_ref.at[col], at_z(d)) for d in (2, 1, 3)}
        gram["partner"] = [send(N_PANEL + 15, gz_ref.at[col], gz_ref.at[col], partner)]

    def gram_forward(d):
        gram["col"][d].wait_recv()
        there = gz_ref.at[piece(4 - d, k)]
        gram["partner"].append(send(N_PANEL + 15 + d, there, there, partner))

    for d in (1, 3, 2):
        ops.append(lambda d=d: gram_forward(d))

    @ops.append
    def _():
        for copy in gram["partner"]:
            copy.wait_recv()
        t_ref[:, :N] = gz_ref[...].reshape(N, N)
        rows_at = lax.broadcasted_iota(jnp.int32, (N, N), 0)
        cols_at = lax.broadcasted_iota(jnp.int32, (N, N), 1)
        t_ref[:, N:] = jnp.where(rows_at == cols_at, 1.0, 0.0).astype(F32)

    sub = lax.broadcasted_iota(jnp.int32, (BLOCK, 128), 0)
    lane = lax.broadcasted_iota(jnp.int32, (BLOCK, 128), 1)
    groups = []

    def tile_of(lo, at):
        e = t_ref[lo:lo + BLOCK, at // 128 * 128:at // 128 * 128 + 128]
        return pltpu.roll(e, 128 - at % 128, 1) if at % 128 else e

    def begin(e):
        e = jnp.where(lane < BLOCK, e, jnp.where(lane == sub + BLOCK, 1.0, 0.0).astype(F32))
        groups[:] = [e[8 * i:8 * i + 8, :] for i in range(BLOCK // 8)]

    def apply(b):
        lo, hi = b * BLOCK, b * BLOCK + BLOCK
        e = jnp.concatenate(groups, axis=0)
        diagonal = jnp.sum(jnp.where(lane == sub, e, 0.0), axis=1, keepdims=True)
        root = lax.rsqrt(diagonal)
        root = root * (1.5 - 0.5 * diagonal * root * root)
        inverse = (e * root)[:, BLOCK:2 * BLOCK]
        if hi < N:
            ahead = dot_nn(inverse, tile_of(lo, hi), HIGHEST)
            begin(tile_of(hi, hi) - dot_tn(ahead[:, :BLOCK], ahead, HIGHEST))
        done = dot_nn(inverse, t_ref[lo:lo + BLOCK, :], HIGHEST)
        t_ref[lo:lo + BLOCK, :] = done
        xh, xl = split(pltpu.roll(done[:, N:], lax.rem(4 - z, 4) * 2 * PIECE, 1))
        ih_out[lo:hi, :] = xh
        il_out[lo:hi, :] = xl
        ah = jnp.concatenate([ab_ref[0, :HALF, :], ab_ref[1, :HALF, :]], axis=0)
        al = jnp.concatenate([ab_ref[0, HALF:, :], ab_ref[1, HALF:, :]], axis=0)
        qh, ql = split((dot_nn(xh, al) + dot_nn(xl, ah)) + dot_nn(xh, ah))
        q_ref[0, lo:hi, :] = qh
        q_ref[1, lo:hi, :] = ql
        if hi < N:
            update = dot_tn(done[:, :N], done, HIGHEST)
            t_ref[hi:, :] -= update[hi:, :]

    @ops.append
    def _():
        rows_at = lax.broadcasted_iota(jnp.int32, (N, N), 0)
        cols_at = lax.broadcasted_iota(jnp.int32, (N, N), 1)
        u_out[...] = jnp.where(cols_at >= rows_at, t_ref[:, :N], 0.0)
        ih, il, qh, ql = ih_out[...], il_out[...], q_ref[0], q_ref[1]
        high, low = split((dot_tn(ih, ql) + dot_tn(il, qh)) + dot_tn(ih, qh))
        bh_out[...] = high
        bl_out[...] = low

    def pieces():
        begin(tile_of(0, 0))
        for b in range(N // BLOCK):
            for g in range(BLOCK // 8):
                eliminate(groups, g)
                if (b == 0 and g == 3) or (b > 0 and g in (1, 4)):
                    yield
            apply(b)
        yield

    work = pieces()
    for n in range(2 * N // BLOCK):
        ops.append(lambda: next(work))

    def rows_of(start, size, align):
        return pl.ds(pl.multiple_of(start, align), size)

    def product(h, d, part):
        where = rows_of(part * 1024 + step(y if part else x, d) * 256, 256, 256)
        both = dot_nt(wh_ref[where, :], ab_ref[h])
        low = dot_nt(wl_ref[where, :], ab_ref[h, :HALF, :])
        c_ref[h, where, :] = (both[:, HALF:] + low) + both[:, :HALF]

    for h in range(2):
        for d in range(4):
            for part in range(2):
                ops.append(lambda h=h, d=d, part=part: product(h, d, part))

    class Stream:
        def __init__(self, h, chunk, part):
            self.h = h
            self.at = (at_y, at_x) if part else (at_x, at_y)
            self.me = (y, x) if part else (x, y)
            self.start = part * 1024 + chunk * S1
            self.number = (h * CHUNKS + chunk) * 2 + part
            self.index = N_PANEL + N_GRAM + self.number * 18
            self.first, self.second, self.back, self.last = {}, {}, {}, {}

        def near(self, d, h):
            start = self.start + step(self.me[0], d) * 256
            return rows_of(start + h * (S1 // 2), S1 // 2, S1 // 2)

        def share(self, d):
            return rows_of(self.start + self.me[0] * 256 + step(self.me[1], d) * S2, S2, S2)

        def sum_out(self, slot, where, d):
            there = r1_ref.at[self.number, slot]
            self.first[slot] = send(self.index + slot, c_ref.at[self.h, where, :], there, self.at[0](d))

        def far_out(self):
            self.sum_out(0, self.near(2, 0), 1)
            self.sum_out(1, self.near(2, 1), 3)

        def near_out(self):
            self.sum_out(2, self.near(1, 1), 1)
            self.sum_out(3, self.near(3, 0), 3)

        def relay(self, slot):
            d = (1, 3)[slot]
            self.first[slot].wait_recv()
            where = self.near(d, slot)
            c_ref[self.h, where, :] += r1_ref[self.number, slot]
            self.sum_out(4 + slot, where, d)

        def turn(self):
            for slot in (2, 3, 4, 5):
                self.first[slot].wait_recv()
            for h, (a, b) in enumerate(((3, 4), (2, 5))):
                where = self.near(0, h)
                c_ref[self.h, where, :] += r1_ref[self.number, a] + r1_ref[self.number, b]
            for d in (2, 1, 3):
                there = r2_ref.at[self.number, d - 1]
                src = c_ref.at[self.h, self.share(d), :]
                self.second[d] = send(self.index + 5 + d, src, there, self.at[1](d))

        def complete(self):
            for d in (1, 2, 3):
                self.second[d].wait_recv()
            where = self.share(0)
            mine = c_ref[self.h, where, :] + r2_ref[self.number, 0]
            f_ref[self.h, where, :] = mine + (r2_ref[self.number, 1] + r2_ref[self.number, 2])
            there = f_ref.at[self.h, where, :]
            for d in (2, 1, 3):
                self.back[d] = send(self.index + 8 + d, there, there, self.at[1](d))

        def spread_out(self, slot, d, h, to):
            there = f_ref.at[self.h, self.near(d, h), :]
            self.last[slot] = send(self.index + 12 + slot, there, there, self.at[0](to))

        def spread(self):
            for d in (1, 2, 3):
                self.back[d].wait_recv()
            self.spread_out(0, 0, 0, 1)
            self.spread_out(1, 0, 1, 3)
            self.spread_out(2, 0, 1, 1)
            self.spread_out(3, 0, 0, 3)

        def hand_on(self, slot):
            self.last[slot].wait_recv()
            self.spread_out(4 + slot, (3, 1)[slot], slot, (1, 3)[slot])

        def end(self):
            for slot in (2, 3, 4, 5):
                self.last[slot].wait_recv()

    for h in range(2):
        for chunk in range(CHUNKS):
            for part in range(2):
                s = Stream(h, chunk, part)
                ops += [s.far_out, s.near_out, lambda s=s: s.relay(0), lambda s=s: s.relay(1), s.turn]
                ops += [s.complete, s.spread, lambda s=s: s.hand_on(0), lambda s=s: s.hand_on(1), s.end]

    assert sorted(ORDER) == list(range(len(ops)))
    for n in ORDER:
        ops[n]()
    for copy in sent:
        copy.wait_send()


def gather_and_factor(panel_cols, window_cols):
    vmem = pl.BlockSpec(memory_space=pltpu.VMEM)
    count = N_PANEL + N_GRAM + N_CROSS
    return pl.pallas_call(
        body,
        out_shape=(
            pltpu.VMEM((N, N), F32),
            pltpu.VMEM((N, N), BF16),
            pltpu.VMEM((N, N), BF16),
            pltpu.VMEM((SLAB, DEPTH), F32),
            pltpu.VMEM((2, SLAB, HALF), F32),
            pltpu.VMEM((N, DEPTH), BF16),
            pltpu.VMEM((N, DEPTH), BF16),
        ),
        in_specs=[pl.BlockSpec(memory_space=pltpu.HBM)] * 2,
        out_specs=(vmem,) * 7,
        scratch_shapes=[
            pltpu.VMEM((PIECE, DEPTH), F32),
            pltpu.VMEM((SLAB, DEPTH), BF16),
            pltpu.VMEM((SLAB, DEPTH), BF16),
            pltpu.VMEM((8, PIECE, DEPTH), F32),
            pltpu.VMEM((2, 2 * HALF, DEPTH), BF16),
            pltpu.VMEM((2, 4, 16, N), F32),
            pltpu.VMEM((2, 4, 16, N), F32),
            pltpu.VMEM((8, PIECE, N), F32),
            pltpu.VMEM((N, 2 * N), F32),
            pltpu.VMEM((2, N, DEPTH), BF16),
            pltpu.VMEM((2, SLAB, HALF), F32),
            pltpu.VMEM((4 * CHUNKS, 6, S1 // 2, HALF), F32),
            pltpu.VMEM((4 * CHUNKS, 3, S2, HALF), F32),
            pltpu.SemaphoreType.DMA((9,)),
            pltpu.SemaphoreType.DMA((count,)),
            pltpu.SemaphoreType.DMA((count,)),
        ],
        compiler_params=pltpu.CompilerParams(
            collective_id=0, has_side_effects=True, vmem_limit_bytes=54900000
        ),
        name="gather_and_factor",
    )(panel_cols, window_cols)


def subtract_body(u_ref, ih_ref, il_ref, w_ref, f_ref, bh_ref, bl_ref, u_out, top_out, out, r_ref, top_ref, sem):
    copies = [pltpu.make_async_copy(u_ref, u_out, sem.at[TILES])]
    copies[0].start()
    rows = SLAB // TILES
    for b in range(TILES):
        where = pl.ds(b * rows, rows)
        fh, fl = split(jnp.concatenate([f_ref[0, where, :], f_ref[1, where, :]], axis=1))
        bh = bh_ref[...]
        r_ref[where, :] = w_ref[where, :] - ((dot_nn(fh, bl_ref[...]) + dot_nn(fl, bh)) + dot_nn(fh, bh))
        copies.append(pltpu.make_async_copy(r_ref.at[where, :], out.at[where, :], sem.at[b]))
        copies[-1].start()
        if b == TILES - 2:
            mine = pl.ds(pl.multiple_of(lax.axis_index("row") * 128, 128), 128)
            fh, fl = split(jnp.concatenate([f_ref[0, mine, :], f_ref[1, mine, :]], axis=1))
            ih = ih_ref[...]
            top_ref[...] = (dot_nt(fh, il_ref[...]) + dot_nt(fl, ih)) + dot_nt(fh, ih)
            copies.append(pltpu.make_async_copy(top_ref, top_out, sem.at[TILES + 1]))
            copies[-1].start()
    for copy in copies:
        copy.wait()


def subtract(*given):
    vmem = pl.BlockSpec(memory_space=pltpu.VMEM)
    anywhere = pl.BlockSpec(memory_space=pl.ANY)
    return pl.pallas_call(
        subtract_body,
        out_shape=(
            jax.ShapeDtypeStruct((N, N), F32),
            jax.ShapeDtypeStruct((128, N), F32),
            jax.ShapeDtypeStruct((SLAB, DEPTH), F32),
        ),
        in_specs=[vmem] * 7,
        out_specs=(anywhere,) * 3,
        scratch_shapes=[
            pltpu.VMEM((SLAB, DEPTH), F32),
            pltpu.VMEM((128, N), F32),
            pltpu.SemaphoreType.DMA((TILES + 2,)),
        ],
        compiler_params=pltpu.CompilerParams(vmem_limit_bytes=24 * 2**20),
        name="subtract",
    )(*given)


def local(panel_cols, window_cols):
    return subtract(*gather_and_factor(panel_cols, window_cols))


def solution(mesh):
    return jax.shard_map(
        local,
        mesh=mesh,
        in_specs=(P("col", "row"), P("col", "row")),
        out_specs=(P(), P(("col", "row"), None), P("col", "row")),
        check_vma=False,
    )
```

```python
import jax
import jax.numpy as jnp
from jax import lax
from jax.experimental import pallas as pl
from jax.experimental.pallas import tpu as pltpu
from jax.sharding import PartitionSpec as P

MESH = pl.DeviceIdType.MESH
HIGHEST = lax.Precision.HIGHEST
F32 = jnp.float32
BF16 = jnp.bfloat16

N = 256
SLAB = 2048
DEPTH = 1024
PIECE = 32
HALF = 128
CHUNKS = 1
S1 = 256 // CHUNKS
S2 = S1 // 4
BLOCK = 64
TILES = 8


ORDER = (
    0, 1, 2, 3, 4, 5, 14, 6, 7, 9, 8, 11, 10, 17, 15, 38, 50, 39, 60, 36, 12, 40, 51, 13, 41, 37, 61, 34, 35, 16, 18,
    46, 70, 47, 80, 42, 43, 44, 52, 53, 62, 63, 49, 48, 71, 45, 81, 19, 72, 73, 82, 83, 54, 64, 20, 74, 84, 55, 65,
    23, 22, 21, 75, 24, 85, 26, 56, 66, 27, 28, 76, 86, 29, 58, 67, 68, 57, 30, 31, 78, 77, 87, 88, 32, 33, 59, 25,
    69, 79, 89,
)


def dot_nt(a, b, precision=None):
    return lax.dot_general(a, b, (((1,), (1,)), ((), ())), precision=precision, preferred_element_type=F32)


def dot_nn(a, b, precision=None):
    return lax.dot_general(a, b, (((1,), (0,)), ((), ())), precision=precision, preferred_element_type=F32)


def dot_tn(a, b, precision=None):
    return lax.dot_general(a, b, (((0,), (0,)), ((), ())), precision=precision, preferred_element_type=F32)


def split(v):
    high = v.astype(BF16)
    return high, (v - high.astype(F32)).astype(BF16)


def spread_row(v, r):
    return jnp.broadcast_to(v[r:r + 1, :], (8, 128))


def spread_lane(v, c):
    return jnp.broadcast_to(v[:, c:c + 1], (8, 128))


def eliminate(groups, g):
    sub = lax.broadcasted_iota(jnp.int32, (8, 128), 0)
    v = groups[g]
    c = [spread_lane(v, 8 * g + t) for t in range(8)]
    w, m = [None] * 8, {}
    for t in range(0, 8, 2):
        r0, r1 = spread_row(v, t), spread_row(v, t + 1)
        p, q, r = spread_row(c[t], t), spread_row(c[t + 1], t), spread_row(c[t + 1], t + 1)
        over = 1.0 / (p * r - q * q)
        po, qo, ro = p * over, q * over, r * over
        w[t], w[t + 1] = ro * r0 - qo * r1, po * r1 - qo * r0
        for u in range(t + 2, 8):
            pu, su = spread_row(c[u], t), spread_row(c[u], t + 1)
            m[t, u], m[t + 1, u] = ro * pu - qo * su, po * su - qo * pu
            c[u] = c[u] - (c[t] * m[t, u] + c[t + 1] * m[t + 1, u])
        new = v - (c[t] * w[t] + c[t + 1] * w[t + 1])
        v = jnp.where(sub > t + 1, new, jnp.where(sub == t + 1, r1 - (q / p) * r0, v))
    groups[g] = v
    if g + 1 == len(groups):
        return
    solved = list(w)
    for t in (4, 2, 0):
        for s in (t, t + 1):
            total = m[s, t + 2] * solved[t + 2]
            for u in range(t + 3, 8):
                total = total + m[s, u] * solved[u]
            solved[s] = w[s] - total
    for i in range(g + 1, len(groups)):
        p = [spread_lane(groups[i], 8 * g + t) * solved[t] for t in range(8)]
        groups[i] = groups[i] - (((p[0] + p[1]) + (p[2] + p[3])) + ((p[4] + p[5]) + (p[6] + p[7])))


N_PANEL = 13
N_GRAM = 19
N_CROSS = 4 * CHUNKS * 18


def body(
    panel_hbm, w_hbm,
    u_out, ih_out, il_out, w_ref, f_ref, bh_out, bl_out,
    panel_ref, wh_ref, wl_ref, a_ref, ab_ref, g1_ref, g2_ref, gz_ref, t_ref,
    q_ref, c_ref, r1_ref, r2_ref, w_sem, send_sem, recv_sem,
):
    row = lax.axis_index("row")
    col = lax.axis_index("col")
    y, x = lax.div(row, 4), lax.rem(row, 4)
    z, k = lax.div(col, 2), lax.rem(col, 2)

    def step(v, d):
        return lax.rem(v + d, 4)

    def at_x(d):
        return (y * 4 + step(x, d), col)

    def at_y(d):
        return (step(y, d) * 4 + x, col)

    def piece(d, core):
        return step(z, d) * 2 + core

    def at_z(d):
        return (row, piece(d, k))

    partner = (row, z * 2 + 1 - k)

    def load_window(b):
        where = pl.ds(b * 256, 256)
        return pltpu.make_async_copy(w_hbm.at[where, :], w_ref.at[where, :], w_sem.at[b])

    load_panel = pltpu.make_async_copy(panel_hbm, panel_ref, w_sem.at[8])
    load_panel.start()
    for b in range(8):
        load_window(b).start()

    barrier = pltpu.get_barrier_semaphore()
    others = [at_x(d) for d in (1, 2, 3)] + [at_y(d) for d in (1, 2, 3)] + [at_z(d) for d in (1, 2, 3)] + [partner]
    for dev in others:
        pl.semaphore_signal(barrier, inc=1, device_id=dev, device_id_type=MESH)
    load_panel.wait()
    pl.semaphore_wait(barrier, len(others))

    sent = []

    def send(index, src, dst, dev):
        copy = pltpu.make_async_remote_copy(
            src_ref=src, dst_ref=dst, send_sem=send_sem.at[index], recv_sem=recv_sem.at[index],
            device_id=dev, device_id_type=MESH,
        )
        copy.start()
        sent.append(copy)
        return copy

    half = (pl.ds(0, 16), pl.ds(16, 16))
    up, down = at_z(1), at_z(3)
    own = {}
    own["up0"] = send(0, panel_ref.at[half[0]], a_ref.at[col, half[0]], up)
    own["down1"] = send(1, panel_ref.at[half[1]], a_ref.at[col, half[1]], down)
    own["up1"] = send(2, panel_ref.at[half[1]], a_ref.at[col, half[1]], up)
    own["down0"] = send(3, panel_ref.at[half[0]], a_ref.at[col, half[0]], down)
    own["partner"] = send(4, panel_ref, a_ref.at[col], partner)
    a_ref[col] = panel_ref[...]

    ops = []

    def split_window(b):
        rows = pl.ds(b * 256, 256)
        load_window(b).wait()
        high, low = split(w_ref[rows, :])
        wh_ref[rows, :] = high
        wl_ref[rows, :] = low

    for b in range(8):
        ops.append(lambda b=b: split_window(b))

    below, above, far = piece(3, k), piece(1, k), piece(2, k)
    gram_blocks = [None] * 4
    passed = {}

    def pass_on(index, who, h, dev):
        return send(index, a_ref.at[who, half[h]], a_ref.at[who, half[h]], dev)

    def pair_here(d, *needs):
        for copy in needs:
            copy.wait_recv()
        pair = a_ref[pl.ds(step(z, d) * 2, 2)].reshape(2 * PIECE, DEPTH)
        high, low = split(pair)
        ab_ref[d // 2, pl.ds(d % 2 * 64, 64), :] = high
        ab_ref[d // 2, pl.ds(HALF + d % 2 * 64, 64), :] = low
        gram_blocks[d] = dot_nt(panel_ref[...], pair, HIGHEST)

    @ops.append
    def _():
        own["down1"].wait_recv()
        passed["relay1"] = pass_on(6, above, 1, down)
        passed["above1"] = pass_on(8, above, 1, partner)

    @ops.append
    def _():
        own["up0"].wait_recv()
        passed["relay0"] = pass_on(5, below, 0, up)
        passed["below0"] = pass_on(7, below, 0, partner)

    @ops.append
    def _():
        own["down0"].wait_recv()
        passed["above0"] = pass_on(10, above, 0, partner)

    @ops.append
    def _():
        own["up1"].wait_recv()
        passed["below1"] = pass_on(9, below, 1, partner)

    @ops.append
    def _():
        passed["relay0"].wait_recv()
        passed["far0"] = pass_on(11, far, 0, partner)

    @ops.append
    def _():
        passed["relay1"].wait_recv()
        passed["far1"] = pass_on(12, far, 1, partner)

    ops.append(lambda: pair_here(0, own["partner"]))
    ops.append(lambda: pair_here(1, passed["above0"], passed["above1"]))
    ops.append(lambda: pair_here(2, passed["far0"], passed["far1"]))
    ops.append(lambda: pair_here(3, passed["below0"], passed["below1"]))

    gram = {}

    @ops.append
    def _():
        slab = pltpu.roll(jnp.concatenate(gram_blocks, axis=1), z * 2 * PIECE, 1)
        gram["first"] = []
        for part, (me, at) in enumerate(((x, at_x), (y, at_y))):
            g1_ref[part, me] = slab[part * 16:part * 16 + 16, :]
            gram["first"] += [
                send(N_PANEL + part * 3 + d - 1, g1_ref.at[part, me], g1_ref.at[part, me], at(d)) for d in (2, 1, 3)
            ]

    def summed(ref, part):
        return (ref[part, 0] + ref[part, 1]) + (ref[part, 2] + ref[part, 3])

    @ops.append
    def _():
        gram["second"] = []
        for part, (me, at) in enumerate(((y, at_y), (x, at_x))):
            for copy in gram["first"][part * 3:part * 3 + 3]:
                copy.wait_recv()
            g2_ref[part, me] = summed(g1_ref, part)
            gram["second"] += [
                send(N_PANEL + 6 + part * 3 + d - 1, g2_ref.at[part, me], g2_ref.at[part, me], at(d)) for d in (2, 1, 3)
            ]

    @ops.append
    def _():
        for part in range(2):
            for copy in gram["second"][part * 3:part * 3 + 3]:
                copy.wait_recv()
            gz_ref[col, part * 16:part * 16 + 16] = summed(g2_ref, part)
        gram["col"] = {d: send(N_PANEL + 12 + d - 1, gz_ref.at[col], gz_ref.at[col], at_z(d)) for d in (2, 1, 3)}
        gram["partner"] = [send(N_PANEL + 15, gz_ref.at[col], gz_ref.at[col], partner)]

    def gram_forward(d):
        gram["col"][d].wait_recv()
        there = gz_ref.at[piece(4 - d, k)]
        gram["partner"].append(send(N_PANEL + 15 + d, there, there, partner))

    for d in (1, 3, 2):
        ops.append(lambda d=d: gram_forward(d))

    @ops.append
    def _():
        for copy in gram["partner"]:
            copy.wait_recv()
        t_ref[:, :N] = gz_ref[...].reshape(N, N)
        rows_at = lax.broadcasted_iota(jnp.int32, (N, N), 0)
        cols_at = lax.broadcasted_iota(jnp.int32, (N, N), 1)
        t_ref[:, N:] = jnp.where(rows_at == cols_at, 1.0, 0.0).astype(F32)

    sub = lax.broadcasted_iota(jnp.int32, (BLOCK, 128), 0)
    lane = lax.broadcasted_iota(jnp.int32, (BLOCK, 128), 1)
    groups = []

    def tile_of(lo, at):
        e = t_ref[lo:lo + BLOCK, at // 128 * 128:at // 128 * 128 + 128]
        return pltpu.roll(e, 128 - at % 128, 1) if at % 128 else e

    def begin(e):
        e = jnp.where(lane < BLOCK, e, jnp.where(lane == sub + BLOCK, 1.0, 0.0).astype(F32))
        groups[:] = [e[8 * i:8 * i + 8, :] for i in range(BLOCK // 8)]

    def apply(b):
        lo, hi = b * BLOCK, b * BLOCK + BLOCK
        e = jnp.concatenate(groups, axis=0)
        diagonal = jnp.sum(jnp.where(lane == sub, e, 0.0), axis=1, keepdims=True)
        root = lax.rsqrt(diagonal)
        root = root * (1.5 - 0.5 * diagonal * root * root)
        inverse = (e * root)[:, BLOCK:2 * BLOCK]
        if hi < N:
            ahead = dot_nn(inverse, tile_of(lo, hi), HIGHEST)
            begin(tile_of(hi, hi) - dot_tn(ahead[:, :BLOCK], ahead, HIGHEST))
        done = dot_nn(inverse, t_ref[lo:lo + BLOCK, :], HIGHEST)
        t_ref[lo:lo + BLOCK, :] = done
        xh, xl = split(pltpu.roll(done[:, N:], lax.rem(4 - z, 4) * 2 * PIECE, 1))
        ih_out[lo:hi, :] = xh
        il_out[lo:hi, :] = xl
        ah = jnp.concatenate([ab_ref[0, :HALF, :], ab_ref[1, :HALF, :]], axis=0)
        al = jnp.concatenate([ab_ref[0, HALF:, :], ab_ref[1, HALF:, :]], axis=0)
        qh, ql = split((dot_nn(xh, al) + dot_nn(xl, ah)) + dot_nn(xh, ah))
        q_ref[0, lo:hi, :] = qh
        q_ref[1, lo:hi, :] = ql
        if hi < N:
            update = dot_tn(done[:, :N], done, HIGHEST)
            t_ref[hi:, :] -= update[hi:, :]

    @ops.append
    def _():
        rows_at = lax.broadcasted_iota(jnp.int32, (N, N), 0)
        cols_at = lax.broadcasted_iota(jnp.int32, (N, N), 1)
        u_out[...] = jnp.where(cols_at >= rows_at, t_ref[:, :N], 0.0)
        ih, il, qh, ql = ih_out[...], il_out[...], q_ref[0], q_ref[1]
        high, low = split((dot_tn(ih, ql) + dot_tn(il, qh)) + dot_tn(ih, qh))
        bh_out[...] = high
        bl_out[...] = low

    def pieces():
        begin(tile_of(0, 0))
        for b in range(N // BLOCK):
            for g in range(BLOCK // 8):
                eliminate(groups, g)
                if (b == 0 and g == 3) or (b > 0 and g in (1, 4)):
                    yield
            apply(b)
        yield

    work = pieces()
    for n in range(2 * N // BLOCK):
        ops.append(lambda: next(work))

    def rows_of(start, size, align):
        return pl.ds(pl.multiple_of(start, align), size)

    def product(h, d, part):
        where = rows_of(part * 1024 + step(y if part else x, d) * 256, 256, 256)
        both = dot_nt(wh_ref[where, :], ab_ref[h])
        low = dot_nt(wl_ref[where, :], ab_ref[h, :HALF, :])
        c_ref[h, where, :] = (both[:, HALF:] + low) + both[:, :HALF]

    for h in range(2):
        for d in range(4):
            for part in range(2):
                ops.append(lambda h=h, d=d, part=part: product(h, d, part))

    class Stream:
        def __init__(self, h, chunk, part):
            self.h = h
            self.at = (at_y, at_x) if part else (at_x, at_y)
            self.me = (y, x) if part else (x, y)
            self.start = part * 1024 + chunk * S1
            self.number = (h * CHUNKS + chunk) * 2 + part
            self.index = N_PANEL + N_GRAM + self.number * 18
            self.first, self.second, self.back, self.last = {}, {}, {}, {}

        def near(self, d, h):
            start = self.start + step(self.me[0], d) * 256
            return rows_of(start + h * (S1 // 2), S1 // 2, S1 // 2)

        def share(self, d):
            return rows_of(self.start + self.me[0] * 256 + step(self.me[1], d) * S2, S2, S2)

        def sum_out(self, slot, where, d):
            there = r1_ref.at[self.number, slot]
            self.first[slot] = send(self.index + slot, c_ref.at[self.h, where, :], there, self.at[0](d))

        def far_out(self):
            self.sum_out(0, self.near(2, 0), 1)
            self.sum_out(1, self.near(2, 1), 3)

        def near_out(self):
            self.sum_out(2, self.near(1, 1), 1)
            self.sum_out(3, self.near(3, 0), 3)

        def relay(self, slot):
            d = (1, 3)[slot]
            self.first[slot].wait_recv()
            where = self.near(d, slot)
            c_ref[self.h, where, :] += r1_ref[self.number, slot]
            self.sum_out(4 + slot, where, d)

        def turn(self):
            for slot in (2, 3, 4, 5):
                self.first[slot].wait_recv()
            for h, (a, b) in enumerate(((3, 4), (2, 5))):
                where = self.near(0, h)
                c_ref[self.h, where, :] += r1_ref[self.number, a] + r1_ref[self.number, b]
            for d in (2, 1, 3):
                there = r2_ref.at[self.number, d - 1]
                src = c_ref.at[self.h, self.share(d), :]
                self.second[d] = send(self.index + 5 + d, src, there, self.at[1](d))

        def complete(self):
            for d in (1, 2, 3):
                self.second[d].wait_recv()
            where = self.share(0)
            mine = c_ref[self.h, where, :] + r2_ref[self.number, 0]
            f_ref[self.h, where, :] = mine + (r2_ref[self.number, 1] + r2_ref[self.number, 2])
            there = f_ref.at[self.h, where, :]
            for d in (2, 1, 3):
                self.back[d] = send(self.index + 8 + d, there, there, self.at[1](d))

        def spread_out(self, slot, d, h, to):
            there = f_ref.at[self.h, self.near(d, h), :]
            self.last[slot] = send(self.index + 12 + slot, there, there, self.at[0](to))

        def spread(self):
            for d in (1, 2, 3):
                self.back[d].wait_recv()
            self.spread_out(0, 0, 0, 1)
            self.spread_out(1, 0, 1, 3)
            self.spread_out(2, 0, 1, 1)
            self.spread_out(3, 0, 0, 3)

        def hand_on(self, slot):
            self.last[slot].wait_recv()
            self.spread_out(4 + slot, (3, 1)[slot], slot, (1, 3)[slot])

        def end(self):
            for slot in (2, 3, 4, 5):
                self.last[slot].wait_recv()

    for h in range(2):
        for chunk in range(CHUNKS):
            for part in range(2):
                s = Stream(h, chunk, part)
                ops += [s.far_out, s.near_out, lambda s=s: s.relay(0), lambda s=s: s.relay(1), s.turn]
                ops += [s.complete, s.spread, lambda s=s: s.hand_on(0), lambda s=s: s.hand_on(1), s.end]

    assert sorted(ORDER) == list(range(len(ops)))
    for n in ORDER:
        ops[n]()
    for copy in sent:
        copy.wait_send()


def gather_and_factor(panel_cols, window_cols):
    vmem = pl.BlockSpec(memory_space=pltpu.VMEM)
    count = N_PANEL + N_GRAM + N_CROSS
    return pl.pallas_call(
        body,
        out_shape=(
            pltpu.VMEM((N, N), F32),
            pltpu.VMEM((N, N), BF16),
            pltpu.VMEM((N, N), BF16),
            pltpu.VMEM((SLAB, DEPTH), F32),
            pltpu.VMEM((2, SLAB, HALF), F32),
            pltpu.VMEM((N, DEPTH), BF16),
            pltpu.VMEM((N, DEPTH), BF16),
        ),
        in_specs=[pl.BlockSpec(memory_space=pltpu.HBM)] * 2,
        out_specs=(vmem,) * 7,
        scratch_shapes=[
            pltpu.VMEM((PIECE, DEPTH), F32),
            pltpu.VMEM((SLAB, DEPTH), BF16),
            pltpu.VMEM((SLAB, DEPTH), BF16),
            pltpu.VMEM((8, PIECE, DEPTH), F32),
            pltpu.VMEM((2, 2 * HALF, DEPTH), BF16),
            pltpu.VMEM((2, 4, 16, N), F32),
            pltpu.VMEM((2, 4, 16, N), F32),
            pltpu.VMEM((8, PIECE, N), F32),
            pltpu.VMEM((N, 2 * N), F32),
            pltpu.VMEM((2, N, DEPTH), BF16),
            pltpu.VMEM((2, SLAB, HALF), F32),
            pltpu.VMEM((4 * CHUNKS, 6, S1 // 2, HALF), F32),
            pltpu.VMEM((4 * CHUNKS, 3, S2, HALF), F32),
            pltpu.SemaphoreType.DMA((9,)),
            pltpu.SemaphoreType.DMA((count,)),
            pltpu.SemaphoreType.DMA((count,)),
        ],
        compiler_params=pltpu.CompilerParams(
            collective_id=0, has_side_effects=True, vmem_limit_bytes=54900000
        ),
        name="gather_and_factor",
    )(panel_cols, window_cols)


def subtract_body(u_ref, ih_ref, il_ref, w_ref, f_ref, bh_ref, bl_ref, u_out, top_out, out, r_ref, top_ref, sem):
    copies = [pltpu.make_async_copy(u_ref, u_out, sem.at[TILES])]
    copies[0].start()
    rows = SLAB // TILES
    for b in range(TILES):
        where = pl.ds(b * rows, rows)
        fh, fl = split(jnp.concatenate([f_ref[0, where, :], f_ref[1, where, :]], axis=1))
        bh = bh_ref[...]
        r_ref[where, :] = w_ref[where, :] - ((dot_nn(fh, bl_ref[...]) + dot_nn(fl, bh)) + dot_nn(fh, bh))
        copies.append(pltpu.make_async_copy(r_ref.at[where, :], out.at[where, :], sem.at[b]))
        copies[-1].start()
        if b == TILES - 2:
            mine = pl.ds(pl.multiple_of(lax.axis_index("row") * 128, 128), 128)
            fh, fl = split(jnp.concatenate([f_ref[0, mine, :], f_ref[1, mine, :]], axis=1))
            ih = ih_ref[...]
            top_ref[...] = (dot_nt(fh, il_ref[...]) + dot_nt(fl, ih)) + dot_nt(fh, ih)
            copies.append(pltpu.make_async_copy(top_ref, top_out, sem.at[TILES + 1]))
            copies[-1].start()
    for copy in copies:
        copy.wait()


def subtract(*given):
    vmem = pl.BlockSpec(memory_space=pltpu.VMEM)
    anywhere = pl.BlockSpec(memory_space=pl.ANY)
    return pl.pallas_call(
        subtract_body,
        out_shape=(
            jax.ShapeDtypeStruct((N, N), F32),
            jax.ShapeDtypeStruct((128, N), F32),
            jax.ShapeDtypeStruct((SLAB, DEPTH), F32),
        ),
        in_specs=[vmem] * 7,
        out_specs=(anywhere,) * 3,
        scratch_shapes=[
            pltpu.VMEM((SLAB, DEPTH), F32),
            pltpu.VMEM((128, N), F32),
            pltpu.SemaphoreType.DMA((TILES + 2,)),
        ],
        compiler_params=pltpu.CompilerParams(vmem_limit_bytes=24 * 2**20),
        name="subtract",
    )(*given)


def local(panel_cols, window_cols):
    return subtract(*gather_and_factor(panel_cols, window_cols))


def solution(mesh):
    return jax.shard_map(
        local,
        mesh=mesh,
        in_specs=(P("col", "row"), P("col", "row")),
        out_specs=(P(), P(("col", "row"), None), P("col", "row")),
        check_vma=False,
    )
```

```python
import jax
import jax.numpy as jnp
from jax import lax
from jax.experimental import pallas as pl
from jax.experimental.pallas import tpu as pltpu
from jax.sharding import PartitionSpec as P

MESH = pl.DeviceIdType.MESH
HIGHEST = lax.Precision.HIGHEST
F32 = jnp.float32
BF16 = jnp.bfloat16

N = 256
SLAB = 2048
DEPTH = 1024
PIECE = 32
HALF = 128
CHUNKS = 1
S1 = 256 // CHUNKS
S2 = S1 // 4
BLOCK = 64
TILES = 8


ORDER = (
    0, 1, 2, 3, 4, 5, 6, 14, 7, 9, 8, 11, 10, 17, 15, 36, 39, 60, 37, 38, 50, 35, 12, 13, 40, 51, 41, 61, 34, 16, 18,
    47, 80, 42, 46, 70, 49, 44, 45, 62, 63, 48, 52, 53, 71, 81, 43, 19, 82, 83, 73, 72, 64, 54, 20, 84, 74, 65, 55,
    23, 21, 22, 85, 75, 24, 26, 66, 56, 27, 28, 86, 76, 29, 68, 58, 67, 57, 30, 31, 87, 88, 78, 77, 32, 33, 25, 69,
    59, 89, 79,
)


def dot_nt(a, b, precision=None):
    return lax.dot_general(a, b, (((1,), (1,)), ((), ())), precision=precision, preferred_element_type=F32)


def dot_nn(a, b, precision=None):
    return lax.dot_general(a, b, (((1,), (0,)), ((), ())), precision=precision, preferred_element_type=F32)


def dot_tn(a, b, precision=None):
    return lax.dot_general(a, b, (((0,), (0,)), ((), ())), precision=precision, preferred_element_type=F32)


def split(v):
    high = v.astype(BF16)
    return high, (v - high.astype(F32)).astype(BF16)


def spread_row(v, r):
    return jnp.broadcast_to(v[r:r + 1, :], (8, 128))


def spread_lane(v, c):
    return jnp.broadcast_to(v[:, c:c + 1], (8, 128))


def eliminate(groups, g):
    sub = lax.broadcasted_iota(jnp.int32, (8, 128), 0)
    v = groups[g]
    c = [spread_lane(v, 8 * g + t) for t in range(8)]
    w, m = [None] * 8, {}
    for t in range(0, 8, 2):
        r0, r1 = spread_row(v, t), spread_row(v, t + 1)
        p, q, r = spread_row(c[t], t), spread_row(c[t + 1], t), spread_row(c[t + 1], t + 1)
        over = 1.0 / (p * r - q * q)
        po, qo, ro = p * over, q * over, r * over
        w[t], w[t + 1] = ro * r0 - qo * r1, po * r1 - qo * r0
        for u in range(t + 2, 8):
            pu, su = spread_row(c[u], t), spread_row(c[u], t + 1)
            m[t, u], m[t + 1, u] = ro * pu - qo * su, po * su - qo * pu
            c[u] = c[u] - (c[t] * m[t, u] + c[t + 1] * m[t + 1, u])
        new = v - (c[t] * w[t] + c[t + 1] * w[t + 1])
        v = jnp.where(sub > t + 1, new, jnp.where(sub == t + 1, r1 - (q / p) * r0, v))
    groups[g] = v
    if g + 1 == len(groups):
        return
    solved = list(w)
    for t in (4, 2, 0):
        for s in (t, t + 1):
            total = m[s, t + 2] * solved[t + 2]
            for u in range(t + 3, 8):
                total = total + m[s, u] * solved[u]
            solved[s] = w[s] - total
    for i in range(g + 1, len(groups)):
        p = [spread_lane(groups[i], 8 * g + t) * solved[t] for t in range(8)]
        groups[i] = groups[i] - (((p[0] + p[1]) + (p[2] + p[3])) + ((p[4] + p[5]) + (p[6] + p[7])))


N_PANEL = 13
N_GRAM = 19
N_CROSS = 4 * CHUNKS * 18


def body(
    panel_hbm, w_hbm,
    u_out, ih_out, il_out, w_ref, f_ref, bh_out, bl_out,
    panel_ref, wh_ref, wl_ref, a_ref, ab_ref, g1_ref, g2_ref, gz_ref, t_ref,
    q_ref, c_ref, r1_ref, r2_ref, w_sem, send_sem, recv_sem,
):
    row = lax.axis_index("row")
    col = lax.axis_index("col")
    y, x = lax.div(row, 4), lax.rem(row, 4)
    z, k = lax.div(col, 2), lax.rem(col, 2)

    def step(v, d):
        return lax.rem(v + d, 4)

    def at_x(d):
        return (y * 4 + step(x, d), col)

    def at_y(d):
        return (step(y, d) * 4 + x, col)

    def piece(d, core):
        return step(z, d) * 2 + core

    def at_z(d):
        return (row, piece(d, k))

    partner = (row, z * 2 + 1 - k)

    def load_window(b):
        where = pl.ds(b * 256, 256)
        return pltpu.make_async_copy(w_hbm.at[where, :], w_ref.at[where, :], w_sem.at[b])

    load_panel = pltpu.make_async_copy(panel_hbm, panel_ref, w_sem.at[8])
    load_panel.start()
    for b in range(8):
        load_window(b).start()

    barrier = pltpu.get_barrier_semaphore()
    others = [at_x(d) for d in (1, 2, 3)] + [at_y(d) for d in (1, 2, 3)] + [at_z(d) for d in (1, 2, 3)] + [partner]
    for dev in others:
        pl.semaphore_signal(barrier, inc=1, device_id=dev, device_id_type=MESH)
    load_panel.wait()
    pl.semaphore_wait(barrier, len(others))

    sent = []

    def send(index, src, dst, dev):
        copy = pltpu.make_async_remote_copy(
            src_ref=src, dst_ref=dst, send_sem=send_sem.at[index], recv_sem=recv_sem.at[index],
            device_id=dev, device_id_type=MESH,
        )
        copy.start()
        sent.append(copy)
        return copy

    half = (pl.ds(0, 16), pl.ds(16, 16))
    up, down = at_z(1), at_z(3)
    own = {}
    own["up0"] = send(0, panel_ref.at[half[0]], a_ref.at[col, half[0]], up)
    own["down1"] = send(1, panel_ref.at[half[1]], a_ref.at[col, half[1]], down)
    own["up1"] = send(2, panel_ref.at[half[1]], a_ref.at[col, half[1]], up)
    own["down0"] = send(3, panel_ref.at[half[0]], a_ref.at[col, half[0]], down)
    own["partner"] = send(4, panel_ref, a_ref.at[col], partner)
    a_ref[col] = panel_ref[...]

    ops = []

    def split_window(b):
        rows = pl.ds(b * 256, 256)
        load_window(b).wait()
        high, low = split(w_ref[rows, :])
        wh_ref[rows, :] = high
        wl_ref[rows, :] = low

    for b in range(8):
        ops.append(lambda b=b: split_window(b))

    below, above, far = piece(3, k), piece(1, k), piece(2, k)
    gram_blocks = [None] * 4
    passed = {}

    def pass_on(index, who, h, dev):
        return send(index, a_ref.at[who, half[h]], a_ref.at[who, half[h]], dev)

    def pair_here(d, *needs):
        for copy in needs:
            copy.wait_recv()
        pair = a_ref[pl.ds(step(z, d) * 2, 2)].reshape(2 * PIECE, DEPTH)
        high, low = split(pair)
        ab_ref[d // 2, pl.ds(d % 2 * 64, 64), :] = high
        ab_ref[d // 2, pl.ds(HALF + d % 2 * 64, 64), :] = low
        gram_blocks[d] = dot_nt(panel_ref[...], pair, HIGHEST)

    @ops.append
    def _():
        own["down1"].wait_recv()
        passed["relay1"] = pass_on(6, above, 1, down)
        passed["above1"] = pass_on(8, above, 1, partner)

    @ops.append
    def _():
        own["up0"].wait_recv()
        passed["relay0"] = pass_on(5, below, 0, up)
        passed["below0"] = pass_on(7, below, 0, partner)

    @ops.append
    def _():
        own["down0"].wait_recv()
        passed["above0"] = pass_on(10, above, 0, partner)

    @ops.append
    def _():
        own["up1"].wait_recv()
        passed["below1"] = pass_on(9, below, 1, partner)

    @ops.append
    def _():
        passed["relay0"].wait_recv()
        passed["far0"] = pass_on(11, far, 0, partner)

    @ops.append
    def _():
        passed["relay1"].wait_recv()
        passed["far1"] = pass_on(12, far, 1, partner)

    ops.append(lambda: pair_here(0, own["partner"]))
    ops.append(lambda: pair_here(1, passed["above0"], passed["above1"]))
    ops.append(lambda: pair_here(2, passed["far0"], passed["far1"]))
    ops.append(lambda: pair_here(3, passed["below0"], passed["below1"]))

    gram = {}

    @ops.append
    def _():
        slab = pltpu.roll(jnp.concatenate(gram_blocks, axis=1), z * 2 * PIECE, 1)
        gram["first"] = []
        for part, (me, at) in enumerate(((x, at_x), (y, at_y))):
            g1_ref[part, me] = slab[part * 16:part * 16 + 16, :]
            gram["first"] += [
                send(N_PANEL + part * 3 + d - 1, g1_ref.at[part, me], g1_ref.at[part, me], at(d)) for d in (2, 1, 3)
            ]

    def summed(ref, part):
        return (ref[part, 0] + ref[part, 1]) + (ref[part, 2] + ref[part, 3])

    @ops.append
    def _():
        gram["second"] = []
        for part, (me, at) in enumerate(((y, at_y), (x, at_x))):
            for copy in gram["first"][part * 3:part * 3 + 3]:
                copy.wait_recv()
            g2_ref[part, me] = summed(g1_ref, part)
            gram["second"] += [
                send(N_PANEL + 6 + part * 3 + d - 1, g2_ref.at[part, me], g2_ref.at[part, me], at(d)) for d in (2, 1, 3)
            ]

    @ops.append
    def _():
        for part in range(2):
            for copy in gram["second"][part * 3:part * 3 + 3]:
                copy.wait_recv()
            gz_ref[col, part * 16:part * 16 + 16] = summed(g2_ref, part)
        gram["col"] = {d: send(N_PANEL + 12 + d - 1, gz_ref.at[col], gz_ref.at[col], at_z(d)) for d in (2, 1, 3)}
        gram["partner"] = [send(N_PANEL + 15, gz_ref.at[col], gz_ref.at[col], partner)]

    def gram_forward(d):
        gram["col"][d].wait_recv()
        there = gz_ref.at[piece(4 - d, k)]
        gram["partner"].append(send(N_PANEL + 15 + d, there, there, partner))

    for d in (1, 3, 2):
        ops.append(lambda d=d: gram_forward(d))

    @ops.append
    def _():
        for copy in gram["partner"]:
            copy.wait_recv()
        t_ref[:, :N] = gz_ref[...].reshape(N, N)
        rows_at = lax.broadcasted_iota(jnp.int32, (N, N), 0)
        cols_at = lax.broadcasted_iota(jnp.int32, (N, N), 1)
        t_ref[:, N:] = jnp.where(rows_at == cols_at, 1.0, 0.0).astype(F32)

    sub = lax.broadcasted_iota(jnp.int32, (BLOCK, 128), 0)
    lane = lax.broadcasted_iota(jnp.int32, (BLOCK, 128), 1)
    groups = []

    def tile_of(lo, at):
        e = t_ref[lo:lo + BLOCK, at // 128 * 128:at // 128 * 128 + 128]
        return pltpu.roll(e, 128 - at % 128, 1) if at % 128 else e

    def begin(e):
        e = jnp.where(lane < BLOCK, e, jnp.where(lane == sub + BLOCK, 1.0, 0.0).astype(F32))
        groups[:] = [e[8 * i:8 * i + 8, :] for i in range(BLOCK // 8)]

    def apply(b):
        lo, hi = b * BLOCK, b * BLOCK + BLOCK
        e = jnp.concatenate(groups, axis=0)
        diagonal = jnp.sum(jnp.where(lane == sub, e, 0.0), axis=1, keepdims=True)
        root = lax.rsqrt(diagonal)
        root = root * (1.5 - 0.5 * diagonal * root * root)
        inverse = (e * root)[:, BLOCK:2 * BLOCK]
        if hi < N:
            ahead = dot_nn(inverse, tile_of(lo, hi), HIGHEST)
            begin(tile_of(hi, hi) - dot_tn(ahead[:, :BLOCK], ahead, HIGHEST))
        done = dot_nn(inverse, t_ref[lo:lo + BLOCK, :], HIGHEST)
        t_ref[lo:lo + BLOCK, :] = done
        xh, xl = split(pltpu.roll(done[:, N:], lax.rem(4 - z, 4) * 2 * PIECE, 1))
        ih_out[lo:hi, :] = xh
        il_out[lo:hi, :] = xl
        ah = jnp.concatenate([ab_ref[0, :HALF, :], ab_ref[1, :HALF, :]], axis=0)
        al = jnp.concatenate([ab_ref[0, HALF:, :], ab_ref[1, HALF:, :]], axis=0)
        qh, ql = split((dot_nn(xh, al) + dot_nn(xl, ah)) + dot_nn(xh, ah))
        q_ref[0, lo:hi, :] = qh
        q_ref[1, lo:hi, :] = ql
        if hi < N:
            update = dot_tn(done[:, :N], done, HIGHEST)
            t_ref[hi:, :] -= update[hi:, :]

    @ops.append
    def _():
        rows_at = lax.broadcasted_iota(jnp.int32, (N, N), 0)
        cols_at = lax.broadcasted_iota(jnp.int32, (N, N), 1)
        u_out[...] = jnp.where(cols_at >= rows_at, t_ref[:, :N], 0.0)
        ih, il, qh, ql = ih_out[...], il_out[...], q_ref[0], q_ref[1]
        high, low = split((dot_tn(ih, ql) + dot_tn(il, qh)) + dot_tn(ih, qh))
        bh_out[...] = high
        bl_out[...] = low

    def pieces():
        begin(tile_of(0, 0))
        for b in range(N // BLOCK):
            for g in range(BLOCK // 8):
                eliminate(groups, g)
                if (b == 0 and g == 3) or (b > 0 and g in (1, 4)):
                    yield
            apply(b)
        yield

    work = pieces()
    for n in range(2 * N // BLOCK):
        ops.append(lambda: next(work))

    def rows_of(start, size, align):
        return pl.ds(pl.multiple_of(start, align), size)

    def product(h, d, part):
        where = rows_of(part * 1024 + step(y if part else x, d) * 256, 256, 256)
        both = dot_nt(wh_ref[where, :], ab_ref[h])
        low = dot_nt(wl_ref[where, :], ab_ref[h, :HALF, :])
        c_ref[h, where, :] = (both[:, HALF:] + low) + both[:, :HALF]

    for h in range(2):
        for d in range(4):
            for part in range(2):
                ops.append(lambda h=h, d=d, part=part: product(h, d, part))

    class Stream:
        def __init__(self, h, chunk, part):
            self.h = h
            self.at = (at_y, at_x) if part else (at_x, at_y)
            self.me = (y, x) if part else (x, y)
            self.start = part * 1024 + chunk * S1
            self.number = (h * CHUNKS + chunk) * 2 + part
            self.index = N_PANEL + N_GRAM + self.number * 18
            self.first, self.second, self.back, self.last = {}, {}, {}, {}

        def near(self, d, h):
            start = self.start + step(self.me[0], d) * 256
            return rows_of(start + h * (S1 // 2), S1 // 2, S1 // 2)

        def share(self, d):
            return rows_of(self.start + self.me[0] * 256 + step(self.me[1], d) * S2, S2, S2)

        def sum_out(self, slot, where, d):
            there = r1_ref.at[self.number, slot]
            self.first[slot] = send(self.index + slot, c_ref.at[self.h, where, :], there, self.at[0](d))

        def far_out(self):
            self.sum_out(0, self.near(2, 0), 1)
            self.sum_out(1, self.near(2, 1), 3)

        def near_out(self):
            self.sum_out(2, self.near(1, 1), 1)
            self.sum_out(3, self.near(3, 0), 3)

        def relay(self, slot):
            d = (1, 3)[slot]
            self.first[slot].wait_recv()
            where = self.near(d, slot)
            c_ref[self.h, where, :] += r1_ref[self.number, slot]
            self.sum_out(4 + slot, where, d)

        def turn(self):
            for slot in (2, 3, 4, 5):
                self.first[slot].wait_recv()
            for h, (a, b) in enumerate(((3, 4), (2, 5))):
                where = self.near(0, h)
                c_ref[self.h, where, :] += r1_ref[self.number, a] + r1_ref[self.number, b]
            for d in (2, 1, 3):
                there = r2_ref.at[self.number, d - 1]
                src = c_ref.at[self.h, self.share(d), :]
                self.second[d] = send(self.index + 5 + d, src, there, self.at[1](d))

        def complete(self):
            for d in (1, 2, 3):
                self.second[d].wait_recv()
            where = self.share(0)
            mine = c_ref[self.h, where, :] + r2_ref[self.number, 0]
            f_ref[self.h, where, :] = mine + (r2_ref[self.number, 1] + r2_ref[self.number, 2])
            there = f_ref.at[self.h, where, :]
            for d in (2, 1, 3):
                self.back[d] = send(self.index + 8 + d, there, there, self.at[1](d))

        def spread_out(self, slot, d, h, to):
            there = f_ref.at[self.h, self.near(d, h), :]
            self.last[slot] = send(self.index + 12 + slot, there, there, self.at[0](to))

        def spread(self):
            for d in (1, 2, 3):
                self.back[d].wait_recv()
            self.spread_out(0, 0, 0, 1)
            self.spread_out(1, 0, 1, 3)
            self.spread_out(2, 0, 1, 1)
            self.spread_out(3, 0, 0, 3)

        def hand_on(self, slot):
            self.last[slot].wait_recv()
            self.spread_out(4 + slot, (3, 1)[slot], slot, (1, 3)[slot])

        def end(self):
            for slot in (2, 3, 4, 5):
                self.last[slot].wait_recv()

    for h in range(2):
        for chunk in range(CHUNKS):
            for part in range(2):
                s = Stream(h, chunk, part)
                ops += [s.far_out, s.near_out, lambda s=s: s.relay(0), lambda s=s: s.relay(1), s.turn]
                ops += [s.complete, s.spread, lambda s=s: s.hand_on(0), lambda s=s: s.hand_on(1), s.end]

    assert sorted(ORDER) == list(range(len(ops)))
    for n in ORDER:
        ops[n]()
    for copy in sent:
        copy.wait_send()


def gather_and_factor(panel_cols, window_cols):
    vmem = pl.BlockSpec(memory_space=pltpu.VMEM)
    count = N_PANEL + N_GRAM + N_CROSS
    return pl.pallas_call(
        body,
        out_shape=(
            pltpu.VMEM((N, N), F32),
            pltpu.VMEM((N, N), BF16),
            pltpu.VMEM((N, N), BF16),
            pltpu.VMEM((SLAB, DEPTH), F32),
            pltpu.VMEM((2, SLAB, HALF), F32),
            pltpu.VMEM((N, DEPTH), BF16),
            pltpu.VMEM((N, DEPTH), BF16),
        ),
        in_specs=[pl.BlockSpec(memory_space=pltpu.HBM)] * 2,
        out_specs=(vmem,) * 7,
        scratch_shapes=[
            pltpu.VMEM((PIECE, DEPTH), F32),
            pltpu.VMEM((SLAB, DEPTH), BF16),
            pltpu.VMEM((SLAB, DEPTH), BF16),
            pltpu.VMEM((8, PIECE, DEPTH), F32),
            pltpu.VMEM((2, 2 * HALF, DEPTH), BF16),
            pltpu.VMEM((2, 4, 16, N), F32),
            pltpu.VMEM((2, 4, 16, N), F32),
            pltpu.VMEM((8, PIECE, N), F32),
            pltpu.VMEM((N, 2 * N), F32),
            pltpu.VMEM((2, N, DEPTH), BF16),
            pltpu.VMEM((2, SLAB, HALF), F32),
            pltpu.VMEM((4 * CHUNKS, 6, S1 // 2, HALF), F32),
            pltpu.VMEM((4 * CHUNKS, 3, S2, HALF), F32),
            pltpu.SemaphoreType.DMA((9,)),
            pltpu.SemaphoreType.DMA((count,)),
            pltpu.SemaphoreType.DMA((count,)),
        ],
        compiler_params=pltpu.CompilerParams(
            collective_id=0, has_side_effects=True, vmem_limit_bytes=54900000
        ),
        name="gather_and_factor",
    )(panel_cols, window_cols)


def subtract_body(u_ref, ih_ref, il_ref, w_ref, f_ref, bh_ref, bl_ref, u_out, top_out, out, r_ref, top_ref, sem):
    copies = [pltpu.make_async_copy(u_ref, u_out, sem.at[TILES])]
    copies[0].start()
    rows = SLAB // TILES
    for b in range(TILES):
        where = pl.ds(b * rows, rows)
        fh, fl = split(jnp.concatenate([f_ref[0, where, :], f_ref[1, where, :]], axis=1))
        bh = bh_ref[...]
        r_ref[where, :] = w_ref[where, :] - ((dot_nn(fh, bl_ref[...]) + dot_nn(fl, bh)) + dot_nn(fh, bh))
        copies.append(pltpu.make_async_copy(r_ref.at[where, :], out.at[where, :], sem.at[b]))
        copies[-1].start()
        if b == TILES - 2:
            mine = pl.ds(pl.multiple_of(lax.axis_index("row") * 128, 128), 128)
            fh, fl = split(jnp.concatenate([f_ref[0, mine, :], f_ref[1, mine, :]], axis=1))
            ih = ih_ref[...]
            top_ref[...] = (dot_nt(fh, il_ref[...]) + dot_nt(fl, ih)) + dot_nt(fh, ih)
            copies.append(pltpu.make_async_copy(top_ref, top_out, sem.at[TILES + 1]))
            copies[-1].start()
    for copy in copies:
        copy.wait()


def subtract(*given):
    vmem = pl.BlockSpec(memory_space=pltpu.VMEM)
    anywhere = pl.BlockSpec(memory_space=pl.ANY)
    return pl.pallas_call(
        subtract_body,
        out_shape=(
            jax.ShapeDtypeStruct((N, N), F32),
            jax.ShapeDtypeStruct((128, N), F32),
            jax.ShapeDtypeStruct((SLAB, DEPTH), F32),
        ),
        in_specs=[vmem] * 7,
        out_specs=(anywhere,) * 3,
        scratch_shapes=[
            pltpu.VMEM((SLAB, DEPTH), F32),
            pltpu.VMEM((128, N), F32),
            pltpu.SemaphoreType.DMA((TILES + 2,)),
        ],
        compiler_params=pltpu.CompilerParams(vmem_limit_bytes=24 * 2**20),
        name="subtract",
    )(*given)


def local(panel_cols, window_cols):
    return subtract(*gather_and_factor(panel_cols, window_cols))


def solution(mesh):
    return jax.shard_map(
        local,
        mesh=mesh,
        in_specs=(P("col", "row"), P("col", "row")),
        out_specs=(P(), P(("col", "row"), None), P("col", "row")),
        check_vma=False,
    )
```
